256 devices in a mesh: grp: 8 (over y_hi, x), head: 32 (over z, y_lo, core).
Axes of the slice: x: 4, y: 4 (y_hi: 2, y_lo: 2; y = y_hi * 2 + y_lo), z: 8, core: 2. Of those that a mesh axis runs over, the one named last changes fastest.
Arguments:
- prefill_token_rows: bfloat16 [512, 8192], P('grp', 'head'), may hold values from -6 to 6
- decode_token_rows: bfloat16 [3, 256, 8192], P(None, 'grp', 'head'), may hold values from -6 to 6
- input_weight: bfloat16 [8192, 8192], P('head'), may hold values from -0.0625 to 0.0625
- lowrank_weight: bfloat16 [8192, 384], P('head'), may hold values from -0.0625 to 0.0625
- step_size_weight: bfloat16 [8192, 64], P('head'), may hold values from -0.0625 to 0.0625
- adapter_up_weight: bfloat16 [128, 4096], P(None, 'head'), may hold values from -1.5 to 1.5
- output_weight: bfloat16 [4096, 8192], P('head'), may hold values from -0.1875 to 0.1875
- head_decay_rate: float32 [64], P('head'), may hold values from 0.0005 to 0.1
- head_step_bias: float32 [64], P('head'), may hold values from -1 to 1
- head_skip_scale: float32 [64], P('head'), may hold values from 0 to 3
- gated_norm_scale: float32 [4096], P('head'), may hold values from 0.1 to 1.9
- prompt_start_state: float32 [16, 64, 64, 128], P('grp', 'head'), may hold values from -18 to 18
- prompt_at_position: int32 [16], replicated, may hold values from 0 to 15, each once
- slot_sample_index: int32 [256], P('grp'), may hold values from 0 to 255, each once
- prompt_adapter_index: int32 [16], replicated, may hold values from 0 to 7
Outputs:
- prefill_out: float32 [512, 8192], P('grp', 'head')
- decode_out: float32 [3, 256, 8192], P(None, 'grp', 'head')
The draws below stay inside these ranges and needn't reach their ends.
Inputs may be any that keep to these rules, and one draw needn't show every extreme that they name: Position i of the prefill rows and of prompt_start_state holds prompt prompt_at_position[i]; every prompt stands once. Decode slot j carries sample slot_sample_index[j] of prompt slot_sample_index[j] // 16; every sample stands once. `prompt_adapter_index`: the adapter used by every row of that prompt and of its samples.
All inputs are finite; a program needn't handle non-finite values.
Results may differ from the reference program's by a relative error of at most 0.0027.
Values may be sent and summed in bfloat16 or wider, within the bound.
A program may use at most 64 MiB of HBM per device.

```python
import math
import jax
import jax.numpy as jnp
from jax import lax

D = 8192
HEAD_CHANNELS = 64
STATE = 128
HEAD_DEV = 2
MIXER_HEADS = 64
INNER_CHANNELS = 4096
STRETCH = 32
PROMPTS = 16
SAMPLES = 16
ROWS = 256
STEPS = 3
ADAPTER_COUNT = 8
ADAPTER_RANK = 16


def with_ends(entries, own_key, least, high):
    spot = [jax.random.randint(jax.random.fold_in(own_key, axis), (), 0, length) for axis, length in enumerate(entries.shape)]
    longest = entries.shape.index(max(entries.shape))
    beside = spot[:longest] + [(spot[longest] + 1) % entries.shape[longest]] + spot[longest + 1:]
    return entries.at[tuple(spot)].set(least).at[tuple(beside)].set(high)


def with_spikes(values, key, source, target, blocks, factor):
    owner, partner = [(jnp.arange(values.shape[dim]) // (values.shape[dim] // blocks)).reshape([-1 if axis == dim else 1 for axis in range(values.ndim)]) for dim in (source, target)]
    chosen = jax.random.permutation(key, blocks)[partner]
    strong = (owner == chosen) | (owner == (partner + blocks // 2) % blocks)
    return jnp.where(strong, factor * values, values)


def steps_of(key, extent, split, smallest, largest):
    factor_of, own = 1.0, jax.random.fold_in(key, 6)
    for axis_at, parts in split:
        heights = jnp.exp(jax.random.uniform(jax.random.fold_in(own, axis_at), (parts,), jnp.float32, smallest / len(split), largest / len(split)))
        factor_of = factor_of * jnp.repeat(heights, extent[axis_at] // parts).reshape([-1 if axis == axis_at else 1 for axis in range(len(extent))])
    return factor_of


def centred(own_key, dims, scale, reach, split=(), kind=jnp.bfloat16):
    values = scale * jax.random.normal(own_key, dims, jnp.float32)
    if split:
        values = values * steps_of(own_key, dims, split, -0.22, 0.18)
    return jnp.clip(values, -reach, reach).astype(kind)


def heavy_noise(own_key, dims, deviation, limit, shards, heavy, kind=jnp.bfloat16):
    drawn = deviation * jax.random.normal(own_key, dims, jnp.float32)
    if shards:
        drawn = drawn * steps_of(own_key, dims, shards, -0.22, 0.18)
    return jnp.clip(with_spikes(drawn, jax.random.fold_in(own_key, 3), *heavy), -limit, limit).astype(kind)


def setup_inputs(seed: int = 0) -> dict:
    key_of = jax.random.split(jax.random.key(seed), 16)
    return {
        "prefill_token_rows": centred(key_of[0], (PROMPTS * STRETCH, D), 1.0, 6.0, ((0, 8), (1, 32))),
        "decode_token_rows": centred(key_of[1], (STEPS, ROWS, D), 1.0, 6.0, ((1, 8), (2, 32))),
        "input_weight": centred(key_of[2], (D, 2 * INNER_CHANNELS), D ** -0.5, 0.0625, ((0, 32),)),
        "lowrank_weight": centred(key_of[3], (D, 2 * STATE + ADAPTER_COUNT * ADAPTER_RANK), D ** -0.5, 0.0625, ((0, 32),)),
        "step_size_weight": centred(key_of[4], (D, MIXER_HEADS), D ** -0.5, 0.0625, ((0, 32),)),
        "adapter_up_weight": centred(key_of[5], (ADAPTER_COUNT * ADAPTER_RANK, INNER_CHANNELS), ADAPTER_RANK ** -0.5, 1.5, ((1, 32),)),
        "output_weight": heavy_noise(key_of[6], (INNER_CHANNELS, D), INNER_CHANNELS ** -0.5, 0.1875, ((0, 32),), (0, 1, 32, 2.75)),
        "head_decay_rate": jnp.clip(jnp.exp(math.log(0.1) - 5.2983173 * jax.random.uniform(key_of[7], (MIXER_HEADS,), jnp.float32) ** steps_of(key_of[7], (MIXER_HEADS,), ((0, 32),), -0.2, 0.2)), 0.0005, 0.1),
        "head_step_bias": jnp.clip(jax.random.uniform(key_of[8], (MIXER_HEADS,), jnp.float32, -1.0, 1.0) * steps_of(key_of[8], (MIXER_HEADS,), ((0, 32),), -0.4, 0.0), -1.0, 1.0),
        "head_skip_scale": jnp.clip(3.0 * jax.random.uniform(key_of[9], (MIXER_HEADS,), jnp.float32) ** steps_of(key_of[9], (MIXER_HEADS,), ((0, 32),), -0.2, 0.2), 0.0, 3.0),
        "gated_norm_scale": jnp.clip(1.0 + 0.18 * jax.random.normal(key_of[10], (INNER_CHANNELS,), jnp.float32), 0.1, 1.9),
        "prompt_start_state": centred(key_of[11], (PROMPTS, MIXER_HEADS, HEAD_CHANNELS, STATE), 3.0, 18.0, ((0, 8), (1, 32)), jnp.float32),
        "prompt_at_position": jax.random.permutation(key_of[12], PROMPTS).astype(jnp.int32),
        "slot_sample_index": jax.random.permutation(key_of[13], ROWS).astype(jnp.int32),
        "prompt_adapter_index": with_ends(jax.random.randint(key_of[14], (PROMPTS,), 0, ADAPTER_COUNT), jax.random.fold_in(key_of[14], 1), 0, ADAPTER_COUNT - 1).astype(jnp.int32),
    }


def block_pass(value_channels, write_vector, read_vector, head_step_length, initial, rate, skip):
    length = value_channels.shape[0]
    log_decay = -(head_step_length * rate[None, :])
    running = jnp.cumsum(log_decay, axis=0).T
    later = jnp.arange(length, dtype=jnp.int32)[:, None] >= jnp.arange(length, dtype=jnp.int32)[None, :]
    spread = jnp.where(later[None], running[:, :, None] - running[:, None, :], 0.0)
    weights = jnp.where(later[None], jnp.exp(spread), 0.0) * head_step_length.T[:, None, :]
    scores = jnp.dot(read_vector, write_vector.T, precision=lax.Precision.HIGHEST)
    mixed = weights * scores[None]
    result = jnp.einsum('hts,shp->thp', mixed, value_channels, precision=lax.Precision.HIGHEST)
    carried = jnp.einsum('hpn,tn->thp', initial, read_vector, precision=lax.Precision.HIGHEST)
    result = result + jnp.exp(running).T[:, :, None] * carried + skip[None, :, None] * value_channels
    ending = running[:, -1]
    tail = jnp.exp(ending[None, :] - running.T) * head_step_length
    final = jnp.exp(ending)[:, None, None] * initial + jnp.einsum('sh,shp,sn->hpn', tail, value_channels, write_vector, precision=lax.Precision.HIGHEST)
    return (result, final)

def prepare_inputs(token_rows, adapter_index, input_weight, lowrank_weight, step_size_weight, adapter_up_weight, head_step_bias):
    token_count = token_rows.shape[0]
    proj = jnp.dot(token_rows, input_weight, preferred_element_type=jnp.float32).reshape(token_count, MIXER_HEADS, 2, HEAD_CHANNELS)
    low = jnp.dot(token_rows, lowrank_weight, preferred_element_type=jnp.float32)
    raw = jnp.dot(token_rows, step_size_weight, preferred_element_type=jnp.float32)
    slot_lanes = jnp.arange(ADAPTER_COUNT * ADAPTER_RANK, dtype=jnp.int32) // ADAPTER_RANK
    selected_rows = jnp.where(slot_lanes[None, :] == adapter_index[:, None], low[:, 2 * STATE:], 0.0).astype(jnp.bfloat16)
    step_delta = jnp.dot(selected_rows, adapter_up_weight, preferred_element_type=jnp.float32).reshape(token_count, MIXER_HEADS, HEAD_CHANNELS)
    value_channels = proj[:, :, 0, :] + step_delta
    gate_branch = proj[:, :, 1, :]
    head_step_length = jax.nn.softplus(raw + head_step_bias[None, :])
    return (value_channels, gate_branch, low[:, :STATE], low[:, STATE:2 * STATE], head_step_length)

def finish(result, gate_branch, token_rows, gated_norm_scale, output_weight):
    token_count = result.shape[0]
    groups = MIXER_HEADS // HEAD_DEV
    width = HEAD_DEV * HEAD_CHANNELS
    gated = (result * jax.nn.silu(gate_branch)).reshape(token_count, groups, width)
    scale = lax.rsqrt(lax.optimization_barrier(jnp.mean(gated * gated, axis=-1, keepdims=True)) + 1e-05)
    normed = (gated * scale * gated_norm_scale.reshape(groups, width)[None]).reshape(token_count, groups * width).astype(jnp.bfloat16)
    summed = jnp.dot(normed, output_weight, preferred_element_type=jnp.float32)
    return token_rows.astype(jnp.float32) + summed

def reference(prefill_token_rows, decode_token_rows, input_weight, lowrank_weight, step_size_weight, adapter_up_weight, output_weight, head_decay_rate, head_step_bias, head_skip_scale, gated_norm_scale, prompt_start_state, prompt_at_position, slot_sample_index, prompt_adapter_index):
    position = jnp.zeros((PROMPTS,), jnp.int32).at[prompt_at_position].set(jnp.arange(PROMPTS, dtype=jnp.int32))
    prefill_tenant_index = jnp.repeat(prompt_adapter_index[prompt_at_position], STRETCH)
    value_channels, gate_branch, write_vector, read_vector, head_step_length = prepare_inputs(prefill_token_rows, prefill_tenant_index, input_weight, lowrank_weight, step_size_weight, adapter_up_weight, head_step_bias)
    shaped = (value_channels.reshape(PROMPTS, STRETCH, MIXER_HEADS, HEAD_CHANNELS), write_vector.reshape(PROMPTS, STRETCH, STATE), read_vector.reshape(PROMPTS, STRETCH, STATE), head_step_length.reshape(PROMPTS, STRETCH, MIXER_HEADS), prompt_start_state)
    results, finals = lax.map(lambda group_args: block_pass(group_args[0], group_args[1], group_args[2], group_args[3], group_args[4], head_decay_rate, head_skip_scale), shaped)
    prefill_out = finish(results.reshape(PROMPTS * STRETCH, MIXER_HEADS, HEAD_CHANNELS), gate_branch, prefill_token_rows, gated_norm_scale, output_weight)
    sample_prompt = slot_sample_index // SAMPLES
    state = finals[position[sample_prompt]]
    row_adapter_index = prompt_adapter_index[sample_prompt]
    outputs = []
    for step in range(STEPS):
        token_rows = decode_token_rows[step]
        value_channels, gate_branch, write_vector, read_vector, head_step_length = prepare_inputs(token_rows, row_adapter_index, input_weight, lowrank_weight, step_size_weight, adapter_up_weight, head_step_bias)
        decay = jnp.exp(-head_step_length * head_decay_rate[None, :])
        state = decay[:, :, None, None] * state + (head_step_length[:, :, None] * value_channels)[:, :, :, None] * write_vector[:, None, None, :]
        result = jnp.einsum('rhpn,rn->rhp', state, read_vector, precision=lax.Precision.HIGHEST) + head_skip_scale[None, :, None] * value_channels
        outputs.append(finish(result, gate_branch, token_rows, gated_norm_scale, output_weight))
    return (prefill_out, jnp.stack(outputs))
```

```python
import jax
import jax.numpy as jnp
from jax import lax
from jax.sharding import PartitionSpec as P

HI = lax.Precision.HIGHEST
F32 = jnp.float32


def iota(shape, dim):
    return lax.broadcasted_iota(jnp.int32, shape, dim)


def dot(a, b, dims=((1,), (0,)), precision=None):
    return lax.dot_general(a, b, (dims, ((), ())), precision=precision, preferred_element_type=F32)


def channels(proj, low, tenant, head_at, up, params):
    rows = proj.shape[0]
    lane = iota((rows, 128), 1)
    picked = jnp.where(lane // 16 == tenant, low[:, 256:384], 0.0).astype(jnp.bfloat16)
    values = jnp.concatenate([proj[:, 0:64], proj[:, 128:192]], axis=1) + dot(picked, up)
    gate = jnp.concatenate([proj[:, 64:128], proj[:, 192:256]], axis=1)
    raw = low[:, 384:512]
    first = jnp.sum(jnp.where(lane == 2 * head_at, raw, 0.0), axis=1, keepdims=True)
    second = jnp.sum(jnp.where(lane == 2 * head_at + 1, raw, 0.0), axis=1, keepdims=True)
    raw = jnp.where(lane < 64, first, second) + params[1:2]
    length = jnp.maximum(raw, 0.0) + jnp.log1p(jnp.exp(-jnp.abs(raw)))
    return values, gate, length, -(length * params[0:1])


def prefill(values, length, decay, writer, reader, start, params):
    rows = values.shape[0]
    t, s = iota((rows, rows), 0), iota((rows, rows), 1)
    keep = (t >= s) & (t // 32 == s // 32)
    running = dot(keep.astype(F32), decay, precision=HI)
    running_t, length_t = running.T, length.T
    scores = dot(reader, writer, ((1,), (1,)), HI)
    parts = []
    for h in range(2):
        spread = running[:, 64 * h : 64 * h + 1] - running_t[64 * h : 64 * h + 1, :]
        weight = jnp.where(keep, jnp.exp(jnp.where(keep, spread, 0.0)), 0.0)
        mixed = weight * length_t[64 * h : 64 * h + 1, :] * scores
        parts.append(dot(mixed, values, precision=HI))
    lane = iota((rows, 128), 1)
    y = jnp.where(lane < 64, parts[0], parts[1]) + params[2:3] * values
    carried, finals = [], []
    for i in range(rows // 32):
        at = slice(32 * i, 32 * i + 32)
        carried.append(dot(reader[at], start[i], ((1,), (1,)), HI))
        last = 32 * i + 31
        tail = jnp.exp(running[last : last + 1] - running[at]) * length[at] * values[at]
        finals.append(jnp.exp(running_t[:, last : last + 1]) * start[i] + dot(tail, writer[at], ((0,), (0,)), HI))
    y = y + jnp.exp(running) * jnp.concatenate(carried, axis=0)
    return y, finals


def decode(values, length, decay, writer, reader, seen, params):
    out, total, totals = [], None, []
    for s in range(3):
        at = slice(32 * s, 32 * s + 32)
        total = decay[at] if total is None else total + decay[at]
        totals.append(total)
        y = jnp.exp(total) * seen[at] + params[2:3] * values[at]
        for u in range(s + 1):
            au = slice(32 * u, 32 * u + 32)
            score = jnp.sum(reader[at] * writer[au], axis=1, keepdims=True)
            term = length[au] * values[au] * score
            y = y + (term if u == s else jnp.exp(total - totals[u]) * term)
        out.append(y)
    return jnp.concatenate(out, axis=0)


def normalise(y, gate, params):
    gated = y * (gate * jax.nn.sigmoid(gate))
    scale = lax.rsqrt(jnp.mean(gated * gated, axis=1, keepdims=True) + 1e-5)
    return (gated * scale * params[3:4]).astype(jnp.bfloat16)


def on_device(pre, dec, w, lw, sw, up, ow, rate, bias, skip, gain, start, at_position, slots, adapter):
    group, head_at = lax.axis_index("grp"), lax.axis_index("head")
    wide = lambda v: jnp.repeat(v, 64)[None]
    params = jnp.concatenate([wide(rate), wide(bias), wide(skip), gain[None]], axis=0)
    rows = jnp.concatenate([pre, dec.reshape(96, 256)], axis=0)
    small = jnp.concatenate([lw, sw, jnp.zeros((256, 64), lw.dtype)], axis=1)
    proj = lax.psum_scatter(dot(w, rows, ((0,), (1,))), "head", scatter_dimension=0, tiled=True).T
    low = lax.psum(dot(rows, small), "head")
    catalog = jnp.arange(16, dtype=jnp.int32)
    held = lax.dynamic_slice_in_dim(at_position, group * 2, 2, 0)
    pick = lambda prompt: jnp.sum(jnp.where(catalog[None] == prompt[:, None], adapter[None], 0), axis=1)
    sample = slots // 16
    tenant = jnp.concatenate([jnp.repeat(pick(held), 32), jnp.tile(pick(sample), 3)])[:, None]
    place = jnp.sum(jnp.where(at_position[None] == sample[:, None], catalog[None], 0), axis=1)
    place = jnp.tile(place, 3)[:, None]
    values, gate, length, decay = channels(proj, low, tenant, head_at, up, params)
    writer, reader = low[:, 0:128], low[:, 128:256]
    y_pre, finals = prefill(
        values[:64], length[:64], decay[:64], writer[:64], reader[:64], start.reshape(2, 128, 128), params
    )
    every = lax.all_gather(jnp.concatenate(finals, axis=0), "grp", axis=0, tiled=True)
    wide_seen = dot(reader[64:], every, ((1,), (1,)), HI)
    seen = jnp.zeros((96, 128), F32)
    for i in range(16):
        seen = jnp.where(place == i, wide_seen[:, 128 * i : 128 * i + 128], seen)
    y_dec = decode(values[64:], length[64:], decay[64:], writer[64:], reader[64:], seen, params)
    normed = normalise(jnp.concatenate([y_pre, y_dec], axis=0), gate, params)
    summed = lax.psum_scatter(dot(ow, normed, ((0,), (1,))), "head", scatter_dimension=0, tiled=True).T
    out = rows.astype(F32) + summed
    return out[:64], out[64:].reshape(3, 32, 256)


def solution(mesh):
    placed = (
        P("grp", "head"),
        P(None, "grp", "head"),
        P("head", None),
        P("head", None),
        P("head", None),
        P(None, "head"),
        P("head", None),
        P("head"),
        P("head"),
        P("head"),
        P("head"),
        P("grp", "head", None, None),
        P(),
        P("grp"),
        P(),
    )
    return jax.shard_map(
        on_device,
        mesh=mesh,
        in_specs=placed,
        out_specs=(P("grp", "head"), P(None, "grp", "head")),
        check_vma=False,
    )
```

```python
import jax
import jax.numpy as jnp
from jax import lax
from jax.experimental import pallas as pl
from jax.experimental.pallas import tpu as pltpu
from jax.sharding import PartitionSpec as P

HI = lax.Precision.HIGHEST
F32 = jnp.float32


def iota(shape, dim):
    return lax.broadcasted_iota(jnp.int32, shape, dim)


def dot(a, b, dims=((1,), (0,)), precision=None):
    return lax.dot_general(a, b, (dims, ((), ())), precision=precision, preferred_element_type=F32)


def channels(proj, low, tenant, head_at, up, params):
    rows = proj.shape[0]
    lane = iota((rows, 128), 1)
    picked = jnp.where(lane // 16 == tenant, low[:, 256:384], 0.0).astype(jnp.bfloat16)
    values = jnp.concatenate([proj[:, 0:64], proj[:, 128:192]], axis=1) + dot(picked, up)
    gate = jnp.concatenate([proj[:, 64:128], proj[:, 192:256]], axis=1)
    raw = low[:, 384:512]
    first = jnp.sum(jnp.where(lane == 2 * head_at, raw, 0.0), axis=1, keepdims=True)
    second = jnp.sum(jnp.where(lane == 2 * head_at + 1, raw, 0.0), axis=1, keepdims=True)
    raw = jnp.where(lane < 64, first, second) + params[1:2]
    length = jnp.maximum(raw, 0.0) + jnp.log1p(jnp.exp(-jnp.abs(raw)))
    return values, gate, length, -(length * params[0:1])


def prefill(values, length, decay, writer, reader, start, params):
    rows = values.shape[0]
    t, s = iota((rows, rows), 0), iota((rows, rows), 1)
    keep = (t >= s) & (t // 32 == s // 32)
    running = dot(keep.astype(F32), decay, precision=HI)
    running_t, length_t = running.T, length.T
    scores = dot(reader, writer, ((1,), (1,)), HI)
    parts = []
    for h in range(2):
        spread = running[:, 64 * h : 64 * h + 1] - running_t[64 * h : 64 * h + 1, :]
        weight = jnp.where(keep, jnp.exp(jnp.where(keep, spread, 0.0)), 0.0)
        mixed = weight * length_t[64 * h : 64 * h + 1, :] * scores
        parts.append(dot(mixed, values, precision=HI))
    lane = iota((rows, 128), 1)
    y = jnp.where(lane < 64, parts[0], parts[1]) + params[2:3] * values
    carried, finals = [], []
    for i in range(rows // 32):
        at = slice(32 * i, 32 * i + 32)
        carried.append(dot(reader[at], start[i], ((1,), (1,)), HI))
        last = 32 * i + 31
        tail = jnp.exp(running[last : last + 1] - running[at]) * length[at] * values[at]
        finals.append(jnp.exp(running_t[:, last : last + 1]) * start[i] + dot(tail.T, writer[at], precision=HI))
    y = y + jnp.exp(running) * jnp.concatenate(carried, axis=0)
    return y, finals


def decode(values, length, decay, writer, reader, seen, params):
    out, total, totals = [], None, []
    for s in range(3):
        at = slice(32 * s, 32 * s + 32)
        total = decay[at] if total is None else total + decay[at]
        totals.append(total)
        y = jnp.exp(total) * seen[at] + params[2:3] * values[at]
        for u in range(s + 1):
            au = slice(32 * u, 32 * u + 32)
            score = jnp.sum(reader[at] * writer[au], axis=1, keepdims=True)
            term = length[au] * values[au] * score
            y = y + (term if u == s else jnp.exp(total - totals[u]) * term)
        out.append(y)
    return jnp.concatenate(out, axis=0)


def normalise(y, gate, params):
    gated = y * (gate * jax.nn.sigmoid(gate))
    scale = lax.rsqrt(jnp.mean(gated * gated, axis=1, keepdims=True) + 1e-5)
    return (gated * scale * params[3:4]).astype(jnp.bfloat16)


def rem(a, n):
    return lax.rem(a, jnp.int32(n))


class Reduce:
    def __init__(self, place, scratch, fill):
        self.z, self.y, self.c = place
        self.part, self.near, self.far, self.out, self.into, self.side, self.sent, self.got = scratch
        self.fill = fill
        self.ready, self.copies = set(), []

    def send(self, source, target, slot, z, y, c):
        return pltpu.make_async_remote_copy(
            src_ref=source,
            dst_ref=target,
            send_sem=self.sent.at[slot],
            recv_sem=self.got.at[slot],
            device_id={"head": z * 4 + y * 2 + c},
            device_id_type=pl.DeviceIdType.MESH,
        )

    def core_copy(self, zp):
        return self.send(self.near.at[zp], self.far.at[zp], zp, self.z, self.y, 1 - self.c)

    def spot(self, i):
        i = jnp.int32(i)
        return rem(self.z + 4 + (1 - 2 * rem(i + 1, 2)) * lax.div(i + 1, jnp.int32(2)), 8)

    def compute(self):
        @pl.loop(0, 8)
        def _(i):
            zp = self.spot(i)
            for yp in range(2):
                self.fill(self.near.at[zp, yp], zp, yp, 1 - self.c)
            self.core_copy(zp).start()

        @pl.loop(0, 8)
        def _(i):
            zp = self.spot(i)
            for yp in range(2):
                self.fill(self.part.at[zp, yp], zp, yp, self.c)

    def need(self, offset):
        zp = rem(self.z + offset, 8)
        if offset not in self.ready:
            self.ready.add(offset)
            self.core_copy(zp).wait_recv()
        return zp

    def hop(self, side, yp, at):
        step = 1 if side else 7
        return self.send(
            self.out.at[side, yp, at],
            self.into.at[side, yp, at],
            8 + side * 8 + yp * 4 + at,
            rem(self.z + step, 8),
            self.y,
            self.c,
        )

    def ring(self, t):
        for side in range(2):
            for yp in range(2):
                first = 4 if side == yp else 3
                away = first - t
                if away < 1:
                    continue
                zp = self.need((away if side else 8 - away) % 8)
                total = self.part[zp, yp] + self.far[zp, yp]
                if away < first:
                    self.hop(side, yp, away).wait_recv()
                    total = total + self.into[side, yp, away].astype(F32)
                self.out[side, yp, away - 1] = total.astype(self.out.dtype)
                copy = self.hop(side, yp, away - 1)
                copy.start()
                self.copies.append(copy)

    def pair(self):
        return self.send(self.side.at[0], self.side.at[1], 24, self.z, 1 - self.y, self.c)

    def gathered(self, yp):
        total = self.part[self.z, yp] + self.far[self.z, yp]
        return total + self.into[0, yp, 0].astype(F32) + self.into[1, yp, 0].astype(F32)

    def across(self):
        self.need(0)
        for side in range(2):
            for yp in range(2):
                self.hop(side, yp, 0).wait_recv()
        self.side[0] = self.gathered(1 - self.y).astype(self.side.dtype)
        self.pair().start()

    def finish(self):
        self.pair().wait_recv()
        return self.gathered(self.y) + self.side[1].astype(F32)

    def drain(self):
        for copy in self.copies:
            copy.wait_send()
        self.pair().wait_send()

        @pl.loop(0, 8)
        def _(i):
            self.core_copy(jnp.int32(i)).wait_send()


def layer(
    pre, dec, w, lw, sw, up, ow, params, start, tags,
    out_pre, out_dec,
    rows, small, low, asked, answer, heard, finals, gates,
    low_sent, low_got, ask_sent, ask_got,
    *scratch,
):
    group, head_at = lax.axis_index("grp"), lax.axis_index("head")
    z, y, c = lax.div(head_at, jnp.int32(4)), rem(lax.div(head_at, jnp.int32(2)), 2), rem(head_at, 2)
    chip = z * 2 + y
    rows[0:64] = pre[...]
    rows[64:160] = dec[...]
    mesh_id = pl.DeviceIdType.MESH

    barrier = pltpu.get_barrier_semaphore()

    @pl.loop(1, 16)
    def _(j):
        pl.semaphore_signal(barrier, 1, device_id={"head": rem(chip + j, 16) * 2 + c}, device_id_type=mesh_id)

    @pl.loop(1, 8)
    def _(j):
        pl.semaphore_signal(barrier, 1, device_id={"grp": rem(group + j, 8)}, device_id_type=mesh_id)

    pl.semaphore_signal(barrier, 1, device_id={"head": chip * 2 + 1 - c}, device_id_type=mesh_id)

    part = dot(rows[...], lw[...])
    small[:, :, 0:384] = part.reshape(10, 16, 384)
    part = dot(rows[...], sw[...])
    small[:, :, 384:512] = jnp.concatenate([part, jnp.zeros_like(part)], axis=1).reshape(10, 16, 128)
    pl.semaphore_wait(barrier, 23)

    def fill_in(ref, zp, yp, cc):
        column = pl.multiple_of((zp * 4 + yp * 2 + cc) * 256, 256)
        ref[0:160] = dot(rows[...], w[:, pl.ds(column, 256)])
        ref[160:176] = small[rem(zp * 2 + yp, 10), :, pl.ds(pl.multiple_of(cc * 256, 256), 256)]

    place = (z, y, c)
    first = Reduce(place, scratch[0:8], fill_in)
    first.compute()
    for t in range(4):
        first.ring(t)
    first.across()
    reduced = first.finish()
    proj, unit = reduced[0:160], reduced[160:176]

    def low_copy(k, slot, to):
        return pltpu.make_async_remote_copy(
            src_ref=low.at[k, slot],
            dst_ref=low.at[k, slot],
            send_sem=low_sent.at[to],
            recv_sem=low_got.at[k, slot],
            device_id={"head": to * 2 + c},
            device_id_type=mesh_id,
        )

    @pl.when(chip < 10)
    def _():
        low[chip, c] = unit

        @pl.loop(1, 16)
        def _(j):
            low_copy(chip, c, rem(chip + j, 16)).start()

    def pass_copy(k, slot):
        return pltpu.make_async_remote_copy(
            src_ref=low.at[k, slot],
            dst_ref=low.at[k, slot],
            send_sem=low_sent.at[16 + k],
            recv_sem=low_got.at[k, slot],
            device_id={"head": chip * 2 + 1 - c},
            device_id_type=mesh_id,
        )

    @pl.loop(0, 10)
    def _(k):
        @pl.when(k != chip)
        def _():
            low_copy(k, c, chip).wait_recv()

        pass_copy(k, c).start()

    @pl.loop(0, 10)
    def _(k):
        pass_copy(k, 1 - c).wait_recv()

    lows = jnp.concatenate([low[:, 0].reshape(160, 256), low[:, 1].reshape(160, 256)], axis=1)

    asked[group, 0:96] = lows[64:160, 128:256]
    asked[group, 96:128] = jnp.broadcast_to(tags[64:96, 1:2].astype(F32), (32, 128))

    def ask(source, g):
        return pltpu.make_async_remote_copy(
            src_ref=asked.at[source],
            dst_ref=asked.at[source],
            send_sem=ask_sent.at[0, g],
            recv_sem=ask_got.at[0, source],
            device_id={"grp": g},
            device_id_type=mesh_id,
        )

    def reply(source, g):
        return pltpu.make_async_remote_copy(
            src_ref=answer.at[g],
            dst_ref=heard.at[source],
            send_sem=ask_sent.at[1, g],
            recv_sem=ask_got.at[1, source],
            device_id={"grp": g},
            device_id_type=mesh_id,
        )

    @pl.loop(1, 8)
    def _(j):
        ask(group, rem(group + j, 8)).start()

    values, gate, length, decay = channels(proj, lows, tags[:, 0:1], head_at, up[...], params)
    writer, reader = lows[:, 0:128], lows[:, 128:256]
    gates[...] = gate[64:160]
    y_pre, ends = prefill(values[:64], length[:64], decay[:64], writer[:64], reader[:64], start, params)
    finals[0:128] = ends[0]
    finals[128:256] = ends[1]

    def serve(g):
        seen = dot(asked[g, 0:96], finals[...], ((1,), (1,)), HI)
        spot = asked[g, 96:128]
        spot = jnp.concatenate([spot, spot, spot], axis=0)
        mine = (2 * group).astype(F32)
        one = jnp.where(spot == mine, seen[:, 0:128], 0.0)
        answer[g] = jnp.where(spot == mine + 1.0, seen[:, 128:256], one)

    @pl.loop(1, 8)
    def _(j):
        g = rem(group + j, 8)
        ask(g, g).wait_recv()
        serve(g)
        reply(group, g).start()

    serve(group)
    normed_pre = normalise(y_pre, gate[0:64], params)

    def fill_out(normed):
        def fill(ref, zp, yp, cc):
            column = pl.multiple_of((zp * 4 + yp * 2 + cc) * 256, 256)
            ref[...] = dot(normed, ow[:, pl.ds(column, 256)])

        return fill

    second = Reduce(place, scratch[8:16], fill_out(normed_pre))
    second.compute()
    second.ring(0)
    second.ring(1)

    heard[group] = answer[group]

    @pl.loop(1, 8)
    def _(j):
        g = rem(group + j, 8)
        reply(g, g).wait_recv()

    seen = heard[0]
    for g in range(1, 8):
        seen = seen + heard[g]
    y_dec = decode(values[64:], length[64:], decay[64:], writer[64:], reader[64:], seen, params)
    normed_dec = normalise(y_dec, gates[...], params)
    third = Reduce(place, scratch[16:24], fill_out(normed_dec))
    third.compute()
    second.ring(2)
    third.ring(0)
    second.ring(3)
    third.ring(1)
    second.across()
    third.ring(2)
    out_pre[...] = second.finish()
    third.ring(3)
    third.across()
    out_dec[...] = third.finish()

    for reduce in (first, second, third):
        reduce.drain()

    @pl.when(chip < 10)
    def _():
        @pl.loop(1, 16)
        def _(j):
            low_copy(chip, c, rem(chip + j, 16)).wait_send()

    @pl.loop(0, 10)
    def _(k):
        pass_copy(k, c).wait_send()

    @pl.loop(1, 8)
    def _(j):
        g = rem(group + j, 8)
        ask(group, g).wait_send()
        reply(group, g).wait_send()


def reduce_scratch(rows, kind):
    return [
        pltpu.VMEM((8, 2, rows, 256), F32),
        pltpu.VMEM((8, 2, rows, 256), F32),
        pltpu.VMEM((8, 2, rows, 256), F32),
        pltpu.VMEM((2, 2, 4, rows, 256), kind),
        pltpu.VMEM((2, 2, 4, rows, 256), kind),
        pltpu.VMEM((2, rows, 256), kind),
        pltpu.SemaphoreType.DMA((25,)),
        pltpu.SemaphoreType.DMA((25,)),
    ]


def on_device(pre, dec, w, lw, sw, up, ow, rate, bias, skip, gain, start, at_position, slots, adapter):
    group = lax.axis_index("grp")
    wide = lambda v: jnp.repeat(v, 64)[None]
    params = jnp.concatenate([wide(rate), wide(bias), wide(skip), gain[None]], axis=0)
    catalog = jnp.arange(16, dtype=jnp.int32)
    held = lax.dynamic_slice_in_dim(at_position, group * 2, 2, 0)
    prompt = jnp.concatenate([jnp.repeat(held, 32), jnp.tile(slots // 16, 3)])
    pick = lambda keys, data: jnp.sum(jnp.where(keys[None] == prompt[:, None], data[None], 0), axis=1, keepdims=True)
    tags = jnp.concatenate([pick(catalog, adapter), pick(at_position, catalog)], axis=1)
    vmem = pl.BlockSpec(memory_space=pltpu.VMEM)
    dec = dec.reshape(96, 256)
    sum_pre, sum_dec = pl.pallas_call(
        layer,
        out_shape=(jax.ShapeDtypeStruct((64, 256), F32), jax.ShapeDtypeStruct((96, 256), F32)),
        in_specs=[vmem] * 10,
        out_specs=(vmem, vmem),
        scratch_shapes=[
            pltpu.VMEM((160, 256), jnp.bfloat16),
            pltpu.VMEM((10, 16, 512), F32),
            pltpu.VMEM((10, 2, 16, 256), F32),
            pltpu.VMEM((8, 128, 128), F32),
            pltpu.VMEM((8, 96, 128), F32),
            pltpu.VMEM((8, 96, 128), F32),
            pltpu.VMEM((256, 128), F32),
            pltpu.VMEM((96, 128), F32),
            pltpu.SemaphoreType.DMA((26,)),
            pltpu.SemaphoreType.DMA((10, 2)),
            pltpu.SemaphoreType.DMA((2, 8)),
            pltpu.SemaphoreType.DMA((2, 8)),
        ]
        + reduce_scratch(176, F32)
        + reduce_scratch(64, jnp.bfloat16)
        + reduce_scratch(96, jnp.bfloat16),
        compiler_params=pltpu.CompilerParams(
            collective_id=0, has_side_effects=True, vmem_limit_bytes=60 * 1024 * 1024
        ),
        name="layer",
    )(pre, dec, w, lw, sw, up, ow, params, start.reshape(2, 128, 128), tags)
    return pre.astype(F32) + sum_pre, (dec.astype(F32) + sum_dec).reshape(3, 32, 256)


def solution(mesh):
    placed = (
        P("grp", "head"),
        P(None, "grp", "head"),
        P("head", None),
        P("head", None),
        P("head", None),
        P(None, "head"),
        P("head", None),
        P("head"),
        P("head"),
        P("head"),
        P("head"),
        P("grp", "head", None, None),
        P(),
        P("grp"),
        P(),
    )
    return jax.shard_map(
        on_device,
        mesh=mesh,
        in_specs=placed,
        out_specs=(P("grp", "head"), P(None, "grp", "head")),
        check_vma=False,
    )
```

```python
import jax
import jax.numpy as jnp
from jax import lax
from jax.experimental import pallas as pl
from jax.experimental.pallas import tpu as pltpu
from jax.sharding import PartitionSpec as P

HI = lax.Precision.HIGHEST
F32 = jnp.float32


def iota(shape, dim):
    return lax.broadcasted_iota(jnp.int32, shape, dim)


def dot(a, b, dims=((1,), (0,)), precision=None):
    return lax.dot_general(a, b, (dims, ((), ())), precision=precision, preferred_element_type=F32)


def rem(a, n):
    return lax.rem(jnp.int32(a), jnp.int32(n))


def div(a, n):
    return lax.div(jnp.int32(a), jnp.int32(n))


def channels(proj, low, tenant, head_at, up, rate, bias):
    rows = proj.shape[0]
    lane = iota((rows, 128), 1)
    picked = jnp.where(lane // 16 == tenant, low[:, 256:384], 0.0).astype(jnp.bfloat16)
    values = jnp.concatenate([proj[:, 0:64], proj[:, 128:192]], axis=1) + dot(picked, up)
    gate = jnp.concatenate([proj[:, 64:128], proj[:, 192:256]], axis=1)
    raw = low[:, 384:512]
    first = jnp.sum(jnp.where(lane == 2 * head_at, raw, 0.0), axis=1, keepdims=True)
    second = jnp.sum(jnp.where(lane == 2 * head_at + 1, raw, 0.0), axis=1, keepdims=True)
    raw = jnp.where(lane < 64, first, second) + bias
    length = jnp.maximum(raw, 0.0) + jnp.log1p(jnp.exp(-jnp.abs(raw)))
    return values, gate, length, -(length * rate)


def causal(rows):
    t, s = iota((rows, rows), 0), iota((rows, rows), 1)
    return (t >= s) & (t // 32 == s // 32)


def run(decay):
    return dot(causal(decay.shape[0]).astype(F32), decay, precision=HI)


def end_states(values, length, running, writer, start):
    running_t = running.T
    out = []
    for i in range(2):
        at = slice(32 * i, 32 * i + 32)
        last = 32 * i + 31
        tail = jnp.exp(running[last : last + 1] - running[at]) * length[at] * values[at]
        out.append(jnp.exp(running_t[:, last : last + 1]) * start[i] + dot(tail.T, writer[at], precision=HI))
    return out


def prefill(values, length, running, writer, reader, start, skip):
    rows = values.shape[0]
    keep = causal(rows)
    running_t, length_t = running.T, length.T
    scores = dot(reader, writer, ((1,), (1,)), HI)
    parts = []
    for h in range(2):
        spread = running[:, 64 * h : 64 * h + 1] - running_t[64 * h : 64 * h + 1, :]
        weight = jnp.where(keep, jnp.exp(jnp.where(keep, spread, 0.0)), 0.0)
        mixed = weight * length_t[64 * h : 64 * h + 1, :] * scores
        parts.append(dot(mixed, values, precision=HI))
    y = jnp.where(iota((rows, 128), 1) < 64, parts[0], parts[1]) + skip * values
    carried = [dot(reader[32 * i : 32 * i + 32], start[i], ((1,), (1,)), HI) for i in range(2)]
    return y + jnp.exp(running) * jnp.concatenate(carried, axis=0)


def decode(values, length, decay, writer, reader, skip):
    out, grown, total, totals = [], [], None, []
    for s in range(3):
        at = slice(32 * s, 32 * s + 32)
        total = decay[at] if total is None else total + decay[at]
        totals.append(total)
        grown.append(jnp.exp(total))
        y = skip * values[at]
        for u in range(s + 1):
            au = slice(32 * u, 32 * u + 32)
            score = jnp.sum(reader[at] * writer[au], axis=1, keepdims=True)
            term = length[au] * values[au] * score
            y = y + (term if u == s else jnp.exp(total - totals[u]) * term)
        out.append(y)
    return jnp.concatenate(out, axis=0), jnp.concatenate(grown, axis=0)


def normalise(y, gate, gain):
    gated = y * (gate * jax.nn.sigmoid(gate))
    scale = lax.rsqrt(jnp.mean(gated * gated, axis=1, keepdims=True) + 1e-5)
    return (gated * scale * gain).astype(jnp.bfloat16)


def encode(v):
    top = jnp.maximum(jnp.max(jnp.abs(v), axis=0, keepdims=True), 1e-30)
    return jnp.round(v * (32767.0 / top)).astype(jnp.int32).astype(jnp.int16), top * (1.0 / 32767.0)


def plain(code, scale):
    return code.astype(jnp.int32).astype(F32) * scale


class Copies:
    def __init__(self, out, into, source, target, sent, got, slot_sent, slot_got, device):
        self.all = [
            pltpu.make_async_remote_copy(
                src_ref=o.at[source],
                dst_ref=i.at[target],
                send_sem=sent.at[n, slot_sent],
                recv_sem=got.at[n, slot_got],
                device_id=device,
                device_id_type=pl.DeviceIdType.MESH,
            )
            for n, (o, i) in enumerate(zip(out, into))
        ]

    def start(self):
        for copy in self.all:
            copy.start()

    def wait_recv(self):
        for copy in self.all:
            copy.wait_recv()

    def wait_send(self):
        for copy in self.all:
            copy.wait_send()


def put(pair, at, v):
    code, scale = encode(v)
    pair[0][at] = code
    pair[1][at] = scale


def get(pair, at):
    return plain(pair[0][at], pair[1][at])


class Base:
    def __init__(self, place, scratch, fill, before=None):
        self.z, self.y, self.c = place
        self.near, self.far, self.part, self.sent, self.got = scratch
        self.fill, self.before = fill, before
        self.ready = set()

    def core_copy(self, zp):
        return pltpu.make_async_remote_copy(
            src_ref=self.near.at[zp],
            dst_ref=self.far.at[zp],
            send_sem=self.sent.at[zp],
            recv_sem=self.got.at[zp],
            device_id={"head": self.z * 4 + self.y * 2 + 1 - self.c},
            device_id_type=pl.DeviceIdType.MESH,
        )

    def spot(self, i):
        return rem(self.z + 4 + (1 - 2 * rem(i, 2)) * div(i + 1, 2), 8)

    def near_of(self, a, b):
        @pl.loop(a, b)
        def _(i):
            zp = self.spot(i)
            if self.before is not None:
                self.before(zp)
            for yp in range(2):
                self.fill(self.near.at[zp, yp], zp, yp, 1 - self.c)
            self.core_copy(zp).start()

    def own_of(self, a, b):
        @pl.loop(a, b)
        def _(i):
            zp = self.spot(i)
            for yp in range(2):
                self.fill(self.part.at[zp, yp], zp, yp, self.c)

    def need(self, offset):
        zp = rem(self.z + offset, 8)
        if offset not in self.ready:
            self.ready.add(offset)
            self.core_copy(zp).wait_recv()
        return zp

    def drain(self):
        @pl.loop(0, 8)
        def _(i):
            self.core_copy(jnp.int32(i)).wait_send()


class Order:
    def __init__(self, base, lo, hi, scratch):
        self.base, self.lo, self.hi = base, lo, hi
        self.z, self.y, self.c = base.z, base.y, base.c
        self.out, self.into = scratch[0:2], scratch[2:4]
        self.side, self.other = scratch[4:6], scratch[6:8]
        self.sent, self.got = scratch[8:10]
        self.copies = []

    def block(self, zp, yp):
        at = (zp, yp, pl.ds(self.lo, self.hi - self.lo))
        return self.base.part[at] + self.base.far[at]

    def hop(self, at, slot, step):
        return Copies(
            self.out, self.into, at, at, self.sent, self.got, slot, slot,
            {"head": rem(self.z + step, 8) * 4 + self.y * 2 + self.c},
        )

    def pair(self, at, slot):
        return Copies(
            self.side, self.other, at, at, self.sent, self.got, slot, slot,
            {"head": self.z * 4 + (1 - self.y) * 2 + self.c},
        )

    def go(self, copy):
        copy.start()
        self.copies.append(copy)

    def drain(self):
        for copy in self.copies:
            copy.wait_send()


class ZFirst(Order):
    def message(self, side, yp, at):
        return self.hop((side, yp, at), side * 8 + yp * 4 + at, 1 if side else 7)

    def ring(self, t):
        for side in range(2):
            for yp in range(2):
                first = 4 if side == yp else 3
                away = first - t
                if away < 1:
                    continue
                total = self.block(self.base.need((away if side else 8 - away) % 8), yp)
                if away < first:
                    self.message(side, yp, away).wait_recv()
                    total = total + get(self.into, (side, yp, away))
                put(self.out, (side, yp, away - 1), total)
                self.go(self.message(side, yp, away - 1))

    def gathered(self, yp):
        return self.block(self.z, yp) + get(self.into, (0, yp, 0)) + get(self.into, (1, yp, 0))

    def across(self):
        self.base.need(0)
        for side in range(2):
            for yp in range(2):
                self.message(side, yp, 0).wait_recv()
        put(self.side, 0, self.gathered(1 - self.y))
        self.go(self.pair(0, 16))

    def finish(self):
        total = self.gathered(self.y)
        self.pair(0, 16).wait_recv()
        return total + get(self.other, 0)


class YFirst(Order):
    def cross(self, *offsets):
        for offset in offsets:
            zp = self.base.need(offset)
            put(self.side, zp, self.block(zp, 1 - self.y))
            self.go(self.pair(zp, 8 + zp))

    def message(self, side, at):
        return self.hop((side, at), side * 4 + at, 1 if side else 7)

    def paired(self, offset):
        zp = rem(self.z + offset, 8)
        total = self.block(zp, self.y)
        self.pair(zp, 8 + zp).wait_recv()
        return total + get(self.other, zp)

    def ring(self, t):
        for side in range(2):
            first = 3 if side else 4
            away = first - t
            if away < 1:
                continue
            total = self.paired((away if side else 8 - away) % 8)
            if away < first:
                self.message(side, away).wait_recv()
                total = total + get(self.into, (side, away))
            put(self.out, (side, away - 1), total)
            self.go(self.message(side, away - 1))

    def finish(self):
        total = self.paired(0)
        for side in range(2):
            self.message(side, 0).wait_recv()
        return total + get(self.into, (0, 0)) + get(self.into, (1, 0))


def layer(
    pre, dec, w_hbm, lw, swt, up, ow_hbm, start_hbm, gain, rates, biases, skips, at_position, slots, adapter,
    out_pre, out_dec,
    w, ow, start, load,
    rows, low_part, low_near, low_far, low_sent, low_got,
    owe, owe_scale, owed, owed_scale, owe_sent, owe_got,
    unit, unit_scale, unit_sent, unit_got, pass_sent, pass_got,
    asked, answer, heard, finals, ask_sent, ask_got,
    base_in, z_in, y_in, base_pre, z_pre, base_dec, y_dec,
):
    group, head_at = lax.axis_index("grp"), lax.axis_index("head")
    z, y, c = div(head_at, 4), rem(div(head_at, 2), 2), rem(head_at, 2)
    chip = z * 2 + y
    place = (z, y, c)
    mesh_id = pl.DeviceIdType.MESH

    def w_copy(zp):
        columns = pl.ds(pl.multiple_of(zp * 1024, 1024), 1024)
        return pltpu.make_async_copy(w_hbm.at[:, columns], w.at[zp], load.at[zp])

    @pl.loop(0, 8)
    def _(i):
        w_copy(rem(z + 4 + (1 - 2 * rem(i, 2)) * div(i + 1, 2), 8)).start()

    ow_copy = pltpu.make_async_copy(ow_hbm, ow, load.at[8])
    start_copy = pltpu.make_async_copy(start_hbm, start, load.at[9])
    start_copy.start()
    ow_copy.start()

    barrier = pltpu.get_barrier_semaphore()

    @pl.loop(1, 16)
    def _(j):
        pl.semaphore_signal(barrier, 1, device_id={"head": rem(chip + j, 16) * 2 + c}, device_id_type=mesh_id)

    @pl.loop(1, 8)
    def _(j):
        pl.semaphore_signal(barrier, 1, device_id={"grp": rem(group + j, 8)}, device_id_type=mesh_id)

    pl.semaphore_signal(barrier, 1, device_id={"head": chip * 2 + 1 - c}, device_id_type=mesh_id)

    rows[0:64] = pre[...]
    rows[64:160] = dec[...]
    part = dot(rows[...], lw[...])
    low_part[0] = part[:, 0:256].reshape(10, 16, 256)
    raw = dot(rows[...], swt[...], ((1,), (1,)))
    low_part[1] = jnp.concatenate([part[:, 256:384], raw, jnp.zeros_like(raw)], axis=1).reshape(10, 16, 256)
    low_near[...] = low_part[1 - c]

    spot = iota((64, 128), 0)
    prompt_pre = jnp.where(spot < 32, at_position[2 * group], at_position[2 * group + 1])
    spot = iota((32, 128), 0)
    prompt_dec = jnp.zeros((32, 128), jnp.int32)
    for j in range(32):
        prompt_dec = jnp.where(spot == j, div(slots[j], 16), prompt_dec)
    tenant_pre = jnp.zeros((64, 128), jnp.int32)
    tenant_dec = jnp.zeros((32, 128), jnp.int32)
    where_dec = jnp.zeros((32, 128), F32)
    for j in range(16):
        tenant_pre = jnp.where(prompt_pre == j, adapter[j], tenant_pre)
        tenant_dec = jnp.where(prompt_dec == j, adapter[j], tenant_dec)
        where_dec = jnp.where(prompt_dec == at_position[j], float(j), where_dec)
    tenant_dec = jnp.concatenate([tenant_dec] * 3, axis=0)
    asked[group, 96:128] = where_dec

    pl.semaphore_wait(barrier, 23)

    low_core = pltpu.make_async_remote_copy(
        src_ref=low_near,
        dst_ref=low_far,
        send_sem=low_sent.at[0],
        recv_sem=low_got.at[0],
        device_id={"head": chip * 2 + 1 - c},
        device_id_type=mesh_id,
    )
    low_core.start()

    def owe_copy(u, source):
        return Copies(
            (owe, owe_scale), (owed, owed_scale), u, source, owe_sent, owe_got, u, source, {"head": u * 2 + c}
        )

    def unit_copy(k, to):
        return Copies(
            (unit, unit_scale), (unit, unit_scale), (k, c), (k, c), unit_sent, unit_got, to, k, {"head": to * 2 + c}
        )

    def pass_copy(k, core):
        return Copies(
            (unit, unit_scale), (unit, unit_scale), (k, core), (k, core), pass_sent, pass_got, k, k,
            {"head": chip * 2 + 1 - c},
        )

    def fill_in(ref, zp, yp, cc):
        columns = pl.ds(pl.multiple_of((yp * 2 + cc) * 256, 256), 256)
        ref[...] = dot(rows[...], w[zp, :, columns])

    base = Base(place, base_in, fill_in, lambda zp: w_copy(zp).wait())
    zs, ys = ZFirst(base, 0, 64, z_in), YFirst(base, 64, 160, y_in)
    base.near_of(0, 3)

    low_core.wait_recv()

    @pl.loop(0, 10)
    def _(u):
        put((owe, owe_scale), u, low_part[c, u] + low_far[u])

        @pl.when(u != chip)
        def _():
            owe_copy(u, chip).start()

    base.near_of(3, 5)
    base.own_of(0, 3)
    zs.ring(0)
    ys.cross(4, 3)
    base.near_of(5, 8)
    base.own_of(3, 5)
    ys.cross(5, 2)
    ys.ring(0)

    @pl.when(chip < 10)
    def _():
        owed[chip] = owe[chip]
        owed_scale[chip] = owe_scale[chip]
        total = get((owed, owed_scale), chip)
        for j in range(1, 16):
            source = rem(chip + j, 16)
            owe_copy(chip, source).wait_recv()
            total = total + get((owed, owed_scale), source)
        put((unit, unit_scale), (chip, c), total)

        @pl.loop(1, 16)
        def _(j):
            unit_copy(chip, rem(chip + j, 16)).start()

    zs.ring(1)
    base.own_of(5, 8)
    ys.cross(6, 1)
    ys.ring(1)
    ys.cross(7, 0)
    zs.ring(2)

    @pl.loop(0, 10)
    def _(k):
        @pl.when(k != chip)
        def _():
            unit_copy(k, chip).wait_recv()

        pass_copy(k, c).start()

    ys.ring(2)
    zs.ring(3)
    ys.ring(3)

    @pl.loop(0, 10)
    def _(k):
        pass_copy(k, 1 - c).wait_recv()

    lows = jnp.concatenate(
        [plain(unit[:, core], unit_scale[:, core]).reshape(160, 256) for core in range(2)], axis=1
    )
    asked[group, 0:96] = lows[64:160, 128:256]

    def ask(source, g):
        return pltpu.make_async_remote_copy(
            src_ref=asked.at[source],
            dst_ref=asked.at[source],
            send_sem=ask_sent.at[0, g],
            recv_sem=ask_got.at[0, source],
            device_id={"grp": g},
            device_id_type=mesh_id,
        )

    def reply(source, g):
        return pltpu.make_async_remote_copy(
            src_ref=answer.at[g],
            dst_ref=heard.at[source],
            send_sem=ask_sent.at[1, g],
            recv_sem=ask_got.at[1, source],
            device_id={"grp": g},
            device_id_type=mesh_id,
        )

    @pl.loop(1, 8)
    def _(j):
        ask(group, rem(group + j, 8)).start()

    zs.across()
    half = iota((1, 128), 1) < 64
    rate = jnp.where(half, rates[0], rates[1])
    bias = jnp.where(half, biases[0], biases[1])
    skip = jnp.where(half, skips[0], skips[1])
    low_pre, low_dec = lows[0:64], lows[64:160]
    values, gate, length, decay = channels(zs.finish(), low_pre, tenant_pre, head_at, up[...], rate, bias)
    running = run(decay)
    start_copy.wait()
    ends = end_states(values, length, running, low_pre[:, 0:128], start)
    finals[0:128] = ends[0]
    finals[128:256] = ends[1]

    def serve(g):
        seen = dot(asked[g, 0:96], finals[...], ((1,), (1,)), HI)
        spot = asked[g, 96:128]
        spot = jnp.concatenate([spot, spot, spot], axis=0)
        mine = (2 * group).astype(F32)
        one = jnp.where(spot == mine, seen[:, 0:128], 0.0)
        return jnp.where(spot == mine + 1.0, seen[:, 128:256], one)

    @pl.loop(1, 8)
    def _(j):
        g = rem(group + j, 8)
        ask(g, g).wait_recv()
        answer[g] = serve(g)
        reply(group, g).start()

    heard[group] = serve(group)
    y_out = prefill(values, length, running, low_pre[:, 0:128], low_pre[:, 128:256], start, skip)
    normed_pre = normalise(y_out, gate, gain[...])

    def fill_out(normed):
        def fill(ref, zp, yp, cc):
            columns = pl.ds(pl.multiple_of((zp * 4 + yp * 2 + cc) * 256, 256), 256)
            ref[...] = dot(normed, ow[:, columns])

        return fill

    ow_copy.wait()
    second_base = Base(place, base_pre, fill_out(normed_pre))
    second = ZFirst(second_base, 0, 64, z_pre)
    second_base.near_of(0, 8)
    second_base.own_of(0, 8)
    second.ring(0)
    values, gate, length, decay = channels(ys.finish(), low_dec, tenant_dec, head_at, up[...], rate, bias)
    y_own, grown = decode(values, length, decay, low_dec[:, 0:128], low_dec[:, 128:256], skip)
    second.ring(1)

    @pl.loop(1, 8)
    def _(j):
        g = rem(group + j, 8)
        reply(g, g).wait_recv()

    seen = heard[0]
    for g in range(1, 8):
        seen = seen + heard[g]
    normed_dec = normalise(y_own + grown * seen, gate, gain[...])
    third_base = Base(place, base_dec, fill_out(normed_dec))
    third = YFirst(third_base, 0, 96, y_dec)
    third_base.near_of(0, 5)
    third_base.own_of(0, 5)
    third.cross(4, 3)
    third_base.near_of(5, 8)
    third.cross(5, 2)
    second.ring(2)
    third.ring(0)
    third_base.own_of(5, 8)
    third.cross(6, 1)
    third.cross(7, 0)
    second.ring(3)
    third.ring(1)
    second.across()
    third.ring(2)
    third.ring(3)
    out_pre[...] = second.finish()
    out_dec[...] = third.finish()

    for order in (base, zs, ys, second_base, second, third_base, third):
        order.drain()
    low_core.wait_send()

    @pl.loop(0, 10)
    def _(k):
        @pl.when(k != chip)
        def _():
            owe_copy(k, chip).wait_send()

        pass_copy(k, c).wait_send()

    @pl.when(chip < 10)
    def _():
        @pl.loop(1, 16)
        def _(j):
            unit_copy(chip, rem(chip + j, 16)).wait_send()

    @pl.loop(1, 8)
    def _(j):
        g = rem(group + j, 8)
        ask(group, g).wait_send()
        reply(group, g).wait_send()


def coded(*lead, rows):
    return [pltpu.VMEM((*lead, rows, 256), jnp.int16), pltpu.VMEM((*lead, 1, 256), F32)]


def base_scratch(rows):
    return [pltpu.VMEM((8, 2, rows, 256), F32)] * 3 + [pltpu.SemaphoreType.DMA((8,))] * 2


def z_scratch(rows):
    return coded(2, 2, 4, rows=rows) * 2 + coded(1, rows=rows) * 2 + [pltpu.SemaphoreType.DMA((2, 17))] * 2


def y_scratch(rows):
    return coded(2, 4, rows=rows) * 2 + coded(8, rows=rows) * 2 + [pltpu.SemaphoreType.DMA((2, 16))] * 2


def on_device(pre, dec, w, lw, sw, up, ow, rate, bias, skip, gain, start, at_position, slots, adapter):
    vmem = pl.BlockSpec(memory_space=pltpu.VMEM)
    smem = pl.BlockSpec(memory_space=pltpu.SMEM)
    any_ = pl.BlockSpec(memory_space=pl.ANY)
    dma = pltpu.SemaphoreType.DMA
    dec = dec.reshape(96, 256)
    sum_pre, sum_dec = pl.pallas_call(
        layer,
        out_shape=(jax.ShapeDtypeStruct((64, 256), F32), jax.ShapeDtypeStruct((96, 256), F32)),
        in_specs=[vmem, vmem, any_, vmem, vmem, vmem, any_, any_, vmem] + [smem] * 6,
        out_specs=(vmem, vmem),
        scratch_shapes=[
            pltpu.VMEM((8, 256, 1024), jnp.bfloat16),
            pltpu.VMEM((128, 8192), jnp.bfloat16),
            pltpu.VMEM((2, 128, 128), F32),
            dma((10,)),
            pltpu.VMEM((160, 256), jnp.bfloat16),
            pltpu.VMEM((2, 10, 16, 256), F32),
            pltpu.VMEM((10, 16, 256), F32),
            pltpu.VMEM((10, 16, 256), F32),
            dma((1,)),
            dma((1,)),
            *coded(10, rows=16),
            *coded(16, rows=16),
            dma((2, 10)),
            dma((2, 16)),
            *coded(10, 2, rows=16),
            dma((2, 16)),
            dma((2, 10)),
            dma((2, 10)),
            dma((2, 10)),
            pltpu.VMEM((8, 128, 128), F32),
            pltpu.VMEM((8, 96, 128), F32),
            pltpu.VMEM((8, 96, 128), F32),
            pltpu.VMEM((256, 128), F32),
            dma((2, 8)),
            dma((2, 8)),
            base_scratch(160),
            z_scratch(64),
            y_scratch(96),
            base_scratch(64),
            z_scratch(64),
            base_scratch(96),
            y_scratch(96),
        ],
        compiler_params=pltpu.CompilerParams(
            collective_id=0, has_side_effects=True, vmem_limit_bytes=60 * 1024 * 1024
        ),
        name="layer",
    )(
        pre, dec, w, lw, sw.T, up, ow, start.reshape(2, 128, 128), gain[None], rate, bias, skip,
        at_position, slots, adapter,
    )
    return pre.astype(F32) + sum_pre, (dec.astype(F32) + sum_dec).reshape(3, 32, 256)


def solution(mesh):
    placed = (
        P("grp", "head"),
        P(None, "grp", "head"),
        P("head", None),
        P("head", None),
        P("head", None),
        P(None, "head"),
        P("head", None),
        P("head"),
        P("head"),
        P("head"),
        P("head"),
        P("grp", "head", None, None),
        P(),
        P("grp"),
        P(),
    )
    return jax.shard_map(
        on_device,
        mesh=mesh,
        in_specs=placed,
        out_specs=(P("grp", "head"), P(None, "grp", "head")),
        check_vma=False,
    )
```

```python
import jax
import jax.numpy as jnp
from jax import lax
from jax.experimental import pallas as pl
from jax.experimental.pallas import tpu as pltpu
from jax.sharding import PartitionSpec as P

HI = lax.Precision.HIGHEST
F32 = jnp.float32
IN_BOUND = 3100.0
OUT_BOUND = 1500.0


def iota(shape, dim):
    return lax.broadcasted_iota(jnp.int32, shape, dim)


def dot(a, b, dims=((1,), (0,)), precision=None):
    return lax.dot_general(a, b, (dims, ((), ())), precision=precision, preferred_element_type=F32)


def rem(a, n):
    return lax.rem(jnp.int32(a), jnp.int32(n))


def div(a, n):
    return lax.div(jnp.int32(a), jnp.int32(n))


def turn(i):
    return 4 + (1 - 2 * rem(i, 2)) * div(i + 1, 2)


def split(v):
    high = v.astype(jnp.bfloat16)
    return high, (v - high.astype(F32)).astype(jnp.bfloat16)


def channels(proj, low, tenant, head_at, up, rate, bias):
    rows = proj.shape[0]
    lane = iota((rows, 128), 1)
    picked = jnp.where(lane // 16 == tenant, low[:, 256:384], 0.0).astype(jnp.bfloat16)
    values = jnp.concatenate([proj[:, 0:64], proj[:, 128:192]], axis=1) + dot(picked, up)
    gate = jnp.concatenate([proj[:, 64:128], proj[:, 192:256]], axis=1)
    raw = low[:, 384:512]
    first = jnp.sum(jnp.where(lane == 2 * head_at, raw, 0.0), axis=1, keepdims=True)
    second = jnp.sum(jnp.where(lane == 2 * head_at + 1, raw, 0.0), axis=1, keepdims=True)
    raw = jnp.where(lane < 64, first, second) + bias
    length = jnp.maximum(raw, 0.0) + jnp.log1p(jnp.exp(-jnp.abs(raw)))
    return values, gate, length, -(length * rate)


def causal(rows):
    t, s = iota((rows, rows), 0), iota((rows, rows), 1)
    return (t >= s) & (t // 32 == s // 32)


def run(decay):
    return dot(causal(decay.shape[0]).astype(F32), decay, precision=HI)


def end_states(values, length, running, writer, start):
    running_t = running.T
    out = []
    for i in range(2):
        at = slice(32 * i, 32 * i + 32)
        last = 32 * i + 31
        tail = jnp.exp(running[last : last + 1] - running[at]) * length[at] * values[at]
        out.append(jnp.exp(running_t[:, last : last + 1]) * start[i] + dot(tail.T, writer[at], precision=HI))
    return out


def prefill(values, length, running, writer, reader, start, skip):
    rows = values.shape[0]
    keep = causal(rows)
    running_t, length_t = running.T, length.T
    scores = dot(reader, writer, ((1,), (1,)), HI)
    parts = []
    for h in range(2):
        spread = running[:, 64 * h : 64 * h + 1] - running_t[64 * h : 64 * h + 1, :]
        weight = jnp.where(keep, jnp.exp(jnp.where(keep, spread, 0.0)), 0.0)
        mixed = weight * length_t[64 * h : 64 * h + 1, :] * scores
        parts.append(dot(mixed, values, precision=HI))
    y = jnp.where(iota((rows, 128), 1) < 64, parts[0], parts[1]) + skip * values
    carried = [dot(reader[32 * i : 32 * i + 32], start[i], ((1,), (1,)), HI) for i in range(2)]
    return y + jnp.exp(running) * jnp.concatenate(carried, axis=0)


def decode(values, length, decay, writer, reader, skip):
    out, grown, total, totals = [], [], None, []
    for s in range(3):
        at = slice(32 * s, 32 * s + 32)
        total = decay[at] if total is None else total + decay[at]
        totals.append(total)
        grown.append(jnp.exp(total))
        y = skip * values[at]
        for u in range(s + 1):
            au = slice(32 * u, 32 * u + 32)
            score = jnp.sum(reader[at] * writer[au], axis=1, keepdims=True)
            term = length[au] * values[au] * score
            y = y + (term if u == s else jnp.exp(total - totals[u]) * term)
        out.append(y)
    return jnp.concatenate(out, axis=0), jnp.concatenate(grown, axis=0)


def normalise(y, gate, gain):
    gated = y * (gate * jax.nn.sigmoid(gate))
    scale = lax.rsqrt(jnp.mean(gated * gated, axis=1, keepdims=True) + 1e-5)
    return (gated * scale * gain).astype(jnp.bfloat16)


def encode(v, bound):
    a = jnp.abs(v) + 1e-30
    a = a * lax.rsqrt(a)
    a = a * lax.rsqrt(a)
    a = a * lax.rsqrt(a)
    a = a * (32767.0 / bound**0.125)
    return jnp.round(jnp.where(v < 0.0, -a, a)).astype(jnp.int32).astype(jnp.int16)


def plain(code, bound):
    a = code.astype(jnp.int32).astype(F32) * (bound**0.125 / 32767.0)
    b = a * a
    return a * jnp.abs(a) * b * (b * b)


class Copies:
    def __init__(self, out, into, source, target, sent, got, slot_sent, slot_got, device):
        self.all = [
            pltpu.make_async_remote_copy(
                src_ref=out.at[source],
                dst_ref=into.at[target],
                send_sem=sent.at[slot_sent],
                recv_sem=got.at[slot_got],
                device_id=device,
                device_id_type=pl.DeviceIdType.MESH,
            )
        ]

    def start(self):
        for copy in self.all:
            copy.start()

    def wait_recv(self):
        for copy in self.all:
            copy.wait_recv()

    def wait_send(self):
        for copy in self.all:
            copy.wait_send()


class Base:
    def __init__(self, place, part, fill):
        self.z, self.y, self.c = place
        self.part, self.fill = part, fill

    def compute(self, a, b):
        @pl.loop(a, b)
        def _(i):
            zp = rem(self.z + turn(i), 8)
            for yp in range(2):
                self.part[zp, yp] = self.fill(zp * 2 + yp)

    def need(self, offset):
        return rem(self.z + offset, 8)


class Order:
    def __init__(self, base, lo, hi, bound, scratch):
        self.base, self.lo, self.hi, self.bound = base, lo, hi, bound
        self.z, self.y, self.c = base.z, base.y, base.c
        self.out, self.into, self.side, self.other, self.sent, self.got = scratch
        self.copies = []

    def block(self, zp, yp):
        at = (zp, yp, pl.ds(self.lo, self.hi - self.lo))
        return self.base.part[at]

    def hop(self, at, slot, step):
        return Copies(
            self.out, self.into, at, at, self.sent, self.got, slot, slot,
            {"head": rem(self.z + step, 8) * 4 + self.y * 2 + self.c},
        )

    def pair(self, at, slot):
        return Copies(
            self.side, self.other, at, at, self.sent, self.got, slot, slot,
            {"head": self.z * 4 + (1 - self.y) * 2 + self.c},
        )

    def put(self, ref, at, v):
        ref[at] = encode(v, self.bound)

    def get(self, ref, at):
        return plain(ref[at], self.bound)

    def go(self, copy):
        copy.start()
        self.copies.append(copy)

    def drain(self):
        for copy in self.copies:
            copy.wait_send()


class ZFirst(Order):
    def message(self, side, yp, at):
        return self.hop((side, yp, at), side * 8 + yp * 4 + at, 1 if side else 7)

    def ring(self, t):
        for side in range(2):
            for yp in range(2):
                first = 4 if side == yp else 3
                away = first - t
                if away < 1:
                    continue
                total = self.block(self.base.need((away if side else 8 - away) % 8), yp)
                if away < first:
                    self.message(side, yp, away).wait_recv()
                    total = total + self.get(self.into, (side, yp, away))
                self.put(self.out, (side, yp, away - 1), total)
                self.go(self.message(side, yp, away - 1))

    def gathered(self, yp):
        return self.block(self.z, yp) + self.get(self.into, (0, yp, 0)) + self.get(self.into, (1, yp, 0))

    def across(self):
        self.base.need(0)
        for side in range(2):
            for yp in range(2):
                self.message(side, yp, 0).wait_recv()
        self.put(self.side, 0, self.gathered(1 - self.y))
        self.go(self.pair(0, 16))

    def finish(self):
        total = self.gathered(self.y)
        self.pair(0, 16).wait_recv()
        return total + self.get(self.other, 0)


class YFirst(Order):
    def cross(self, *offsets):
        for offset in offsets:
            zp = self.base.need(offset)
            self.put(self.side, zp, self.block(zp, 1 - self.y))
            self.go(self.pair(zp, 8 + zp))

    def message(self, side, at):
        return self.hop((side, at), side * 4 + at, 1 if side else 7)

    def paired(self, offset):
        zp = rem(self.z + offset, 8)
        total = self.block(zp, self.y)
        self.pair(zp, 8 + zp).wait_recv()
        return total + self.get(self.other, zp)

    def ring(self, t):
        for side in range(2):
            first = 3 if side else 4
            away = first - t
            if away < 1:
                continue
            total = self.paired((away if side else 8 - away) % 8)
            if away < first:
                self.message(side, away).wait_recv()
                total = total + self.get(self.into, (side, away))
            self.put(self.out, (side, away - 1), total)
            self.go(self.message(side, away - 1))

    def finish(self):
        total = self.paired(0)
        for side in range(2):
            self.message(side, 0).wait_recv()
        return total + self.get(self.into, (0, 0)) + self.get(self.into, (1, 0))


def layer(
    pre, dec, w_hbm, lw, swt, up, ow_hbm, start_hbm, gain, rates, biases, skips, at_position, slots, adapter,
    out_pre, out_dec,
    w, ow, start, load, w_sent, w_got,
    rows, low_part, low_near, low_far, low_sent, low_got,
    owe, owed, owe_sent, owe_got,
    unit, unit_sent, unit_got, pass_sent, pass_got,
    asked, answer, heard, finals, ask_sent, ask_got,
    norm_pre, norm_dec, base_in, z_in, y_in, base_pre, z_pre, base_dec, y_dec,
):
    group, head_at = lax.axis_index("grp"), lax.axis_index("head")
    z, y, c = div(head_at, 4), rem(div(head_at, 2), 2), rem(head_at, 2)
    chip = z * 2 + y
    place = (z, y, c)
    mesh_id = pl.DeviceIdType.MESH

    def columns(block, core):
        return pl.ds(pl.multiple_of((block * 2 + core) * 256, 256), 256)

    def w_own(b):
        return pltpu.make_async_copy(w_hbm.at[:, columns(b, c)], w.at[b, 0], load.at[b])

    def ow_own(b):
        return pltpu.make_async_copy(ow_hbm.at[:, columns(b, c)], ow.at[b, 0], load.at[16 + b])

    def to_core(source, target, slot):
        return pltpu.make_async_remote_copy(
            src_ref=source,
            dst_ref=target,
            send_sem=w_sent.at[slot],
            recv_sem=w_got.at[slot],
            device_id={"head": chip * 2 + 1 - c},
            device_id_type=mesh_id,
        )

    def w_other(b):
        return to_core(w_hbm.at[:, columns(b, 1 - c)], w.at[b, 1], b)

    def ow_other(b):
        return to_core(ow_hbm.at[:, columns(b, 1 - c)], ow.at[b, 1], 16 + b)

    pre_other = to_core(pre, rows.at[1, pl.ds(0, 64)], 32)
    dec_other = to_core(dec, rows.at[1, pl.ds(64, 96)], 33)
    normed_pre_other = to_core(norm_pre.at[0], norm_pre.at[1], 34)
    normed_dec_other = to_core(norm_dec.at[0], norm_dec.at[1], 35)

    @pl.loop(0, 8)
    def _(i):
        for yp in range(2):
            w_own(rem(z + turn(i), 8) * 2 + yp).start()

    start_copy = pltpu.make_async_copy(start_hbm, start, load.at[32])
    start_copy.start()

    barrier = pltpu.get_barrier_semaphore()

    @pl.loop(1, 16)
    def _(j):
        pl.semaphore_signal(barrier, 1, device_id={"head": rem(chip + j, 16) * 2 + c}, device_id_type=mesh_id)

    @pl.loop(1, 8)
    def _(j):
        pl.semaphore_signal(barrier, 1, device_id={"grp": rem(group + j, 8)}, device_id_type=mesh_id)

    pl.semaphore_signal(barrier, 1, device_id={"head": chip * 2 + 1 - c}, device_id_type=mesh_id)

    @pl.loop(0, 16)
    def _(b):
        ow_own(b).start()

    rows[0, 0:64] = pre[...]
    rows[0, 64:160] = dec[...]
    part = dot(rows[0], lw[...])
    low_part[0] = part[:, 0:256].reshape(10, 16, 256)
    raw = dot(rows[0], swt[...], ((1,), (1,)))
    low_part[1] = jnp.concatenate([part[:, 256:384], raw, jnp.zeros_like(raw)], axis=1).reshape(10, 16, 256)
    low_near[...] = low_part[1 - c]

    spot = iota((64, 128), 0)
    prompt_pre = jnp.where(spot < 32, at_position[2 * group], at_position[2 * group + 1])
    spot = iota((32, 128), 0)
    prompt_dec = jnp.zeros((32, 128), jnp.int32)
    for j in range(32):
        prompt_dec = jnp.where(spot == j, div(slots[j], 16), prompt_dec)
    tenant_pre = jnp.zeros((64, 128), jnp.int32)
    tenant_dec = jnp.zeros((32, 128), jnp.int32)
    where_dec = jnp.zeros((32, 128), F32)
    for j in range(16):
        tenant_pre = jnp.where(prompt_pre == j, adapter[j], tenant_pre)
        tenant_dec = jnp.where(prompt_dec == j, adapter[j], tenant_dec)
        where_dec = jnp.where(prompt_dec == at_position[j], float(j), where_dec)
    tenant_dec = jnp.concatenate([tenant_dec] * 3, axis=0)
    asked[group, 96:128] = where_dec

    pl.semaphore_wait(barrier, 23)
    pre_other.start()
    dec_other.start()

    @pl.loop(0, 8)
    def _(i):
        for yp in range(2):
            w_other(rem(z + turn(i), 8) * 2 + yp).start()

    low_core = pltpu.make_async_remote_copy(
        src_ref=low_near,
        dst_ref=low_far,
        send_sem=low_sent.at[0],
        recv_sem=low_got.at[0],
        device_id={"head": chip * 2 + 1 - c},
        device_id_type=mesh_id,
    )
    low_core.start()

    def owe_copy(u, source):
        return Copies(
            owe, owed, u, source, owe_sent, owe_got, u, source, {"head": u * 2 + c}
        )

    def unit_copy(k, to):
        return Copies(
            unit, unit, (k, c), (k, c), unit_sent, unit_got, to, k, {"head": to * 2 + c}
        )

    def pass_copy(k, core):
        return Copies(
            unit, unit, (k, core), (k, core), pass_sent, pass_got, k, k,
            {"head": chip * 2 + 1 - c},
        )

    def fill_in(b):
        w_own(b).wait()
        w_other(b).wait_recv()
        both = jnp.concatenate([rows[0], rows[1]], axis=1)
        return dot(both, w[b].reshape(512, 256))

    base = Base(place, base_in, fill_in)
    zs, ys = ZFirst(base, 0, 64, IN_BOUND, z_in), YFirst(base, 64, 160, IN_BOUND, y_in)
    pre_other.wait_recv()
    dec_other.wait_recv()
    base.compute(0, 3)
    zs.ring(0)
    ys.cross(4, 3)
    low_core.wait_recv()

    @pl.loop(0, 10)
    def _(u):
        owe[u] = encode(low_part[c, u] + low_far[u], IN_BOUND)

        @pl.when(u != chip)
        def _():
            owe_copy(u, chip).start()

    base.compute(3, 5)
    ys.cross(5, 2)
    ys.ring(0)

    @pl.when(chip < 10)
    def _():
        owed[chip] = owe[chip]
        total = plain(owed[chip], IN_BOUND)
        for j in range(1, 16):
            source = rem(chip + j, 16)
            owe_copy(chip, source).wait_recv()
            total = total + plain(owed[source], IN_BOUND)
        unit[chip, c] = encode(total, IN_BOUND)

        @pl.loop(1, 16)
        def _(j):
            unit_copy(chip, rem(chip + j, 16)).start()

    zs.ring(1)

    @pl.loop(0, 16)
    def _(b):
        ow_other(b).start()

    base.compute(5, 8)
    ys.cross(6, 1)
    ys.ring(1)
    ys.cross(7, 0)
    zs.ring(2)

    @pl.loop(0, 10)
    def _(k):
        @pl.when(k != chip)
        def _():
            unit_copy(k, chip).wait_recv()

        pass_copy(k, c).start()

    ys.ring(2)
    zs.ring(3)
    ys.ring(3)

    @pl.loop(0, 10)
    def _(k):
        pass_copy(k, 1 - c).wait_recv()

    lows = jnp.concatenate(
        [plain(unit[:, core], IN_BOUND).reshape(160, 256) for core in range(2)], axis=1
    )
    asked[group, 0:96] = lows[64:160, 128:256]

    def ask(source, g):
        return pltpu.make_async_remote_copy(
            src_ref=asked.at[source],
            dst_ref=asked.at[source],
            send_sem=ask_sent.at[0, g],
            recv_sem=ask_got.at[0, source],
            device_id={"grp": g},
            device_id_type=mesh_id,
        )

    def reply(source, g):
        return pltpu.make_async_remote_copy(
            src_ref=answer.at[g],
            dst_ref=heard.at[source],
            send_sem=ask_sent.at[1, g],
            recv_sem=ask_got.at[1, source],
            device_id={"grp": g},
            device_id_type=mesh_id,
        )

    @pl.loop(1, 8)
    def _(j):
        ask(group, rem(group + j, 8)).start()

    zs.across()
    half = iota((1, 128), 1) < 64
    rate = jnp.where(half, rates[0], rates[1])
    bias = jnp.where(half, biases[0], biases[1])
    skip = jnp.where(half, skips[0], skips[1])
    low_pre, low_dec = lows[0:64], lows[64:160]
    values, gate, length, decay = channels(zs.finish(), low_pre, tenant_pre, head_at, up[...], rate, bias)
    running = run(decay)
    start_copy.wait()
    ends = end_states(values, length, running, low_pre[:, 0:128], start)
    finals[0:128] = ends[0]
    finals[128:256] = ends[1]

    @pl.loop(1, 8)
    def _(j):
        g = rem(group + j, 8)
        ask(g, g).wait_recv()

    high, rest = split(asked[:, 0:96].reshape(768, 128))
    state_high, state_rest = split(finals[...])
    across = ((1,), (1,))
    seen = dot(high, state_high, across) + (dot(high, state_rest, across) + dot(rest, state_high, across))
    mine = (2 * group).astype(F32)
    for g in range(8):
        at = slice(96 * g, 96 * g + 96)
        spot = asked[g, 96:128]
        spot = jnp.concatenate([spot, spot, spot], axis=0)
        one = jnp.where(spot == mine, seen[at, 0:128], 0.0)
        answer[g] = jnp.where(spot == mine + 1.0, seen[at, 128:256], one)

    @pl.loop(1, 8)
    def _(j):
        reply(group, rem(group + j, 8)).start()

    heard[group] = answer[group]
    y_out = prefill(values, length, running, low_pre[:, 0:128], low_pre[:, 128:256], start, skip)
    norm_pre[0] = normalise(y_out, gate, gain[...])
    normed_pre_other.start()

    def fill_out(normed):
        def fill(b):
            return dot(jnp.concatenate([normed[0], normed[1]], axis=1), ow[b].reshape(256, 256))

        return fill

    @pl.loop(0, 16)
    def _(b):
        ow_own(b).wait()
        ow_other(b).wait_recv()

    second_base = Base(place, base_pre, fill_out(norm_pre))
    second = ZFirst(second_base, 0, 64, OUT_BOUND, z_pre)
    normed_pre_other.wait_recv()
    second_base.compute(0, 3)
    second.ring(0)
    second_base.compute(3, 8)
    values, gate, length, decay = channels(ys.finish(), low_dec, tenant_dec, head_at, up[...], rate, bias)
    y_own, grown = decode(values, length, decay, low_dec[:, 0:128], low_dec[:, 128:256], skip)
    second.ring(1)

    @pl.loop(1, 8)
    def _(j):
        g = rem(group + j, 8)
        reply(g, g).wait_recv()

    seen = heard[0]
    for g in range(1, 8):
        seen = seen + heard[g]
    norm_dec[0] = normalise(y_own + grown * seen, gate, gain[...])
    normed_dec_other.start()
    third_base = Base(place, base_dec, fill_out(norm_dec))
    third = YFirst(third_base, 0, 96, OUT_BOUND, y_dec)
    second.ring(2)
    normed_dec_other.wait_recv()
    third_base.compute(0, 2)
    third.cross(4, 3)
    third_base.compute(2, 4)
    third.cross(5, 2)
    third_base.compute(4, 8)
    third.cross(6, 1)
    third.ring(0)
    third.cross(7, 0)
    second.ring(3)
    third.ring(1)
    second.across()
    third.ring(2)
    third.ring(3)
    out_pre[...] = second.finish()
    out_dec[...] = third.finish()

    for order in (zs, ys, second, third):
        order.drain()
    for copy in (pre_other, dec_other, normed_pre_other, normed_dec_other):
        copy.wait_send()

    @pl.loop(0, 16)
    def _(b):
        w_other(b).wait_send()
        ow_other(b).wait_send()

    low_core.wait_send()

    @pl.loop(0, 10)
    def _(k):
        @pl.when(k != chip)
        def _():
            owe_copy(k, chip).wait_send()

        pass_copy(k, c).wait_send()

    @pl.when(chip < 10)
    def _():
        @pl.loop(1, 16)
        def _(j):
            unit_copy(chip, rem(chip + j, 16)).wait_send()

    @pl.loop(1, 8)
    def _(j):
        g = rem(group + j, 8)
        ask(group, g).wait_send()
        reply(group, g).wait_send()


def coded(*lead, rows):
    return [pltpu.VMEM((*lead, rows, 256), jnp.int16)]


def base_scratch(rows):
    return pltpu.VMEM((8, 2, rows, 256), F32)


def z_scratch(rows):
    return coded(2, 2, 4, rows=rows) * 2 + coded(1, rows=rows) * 2 + [pltpu.SemaphoreType.DMA((17,))] * 2


def y_scratch(rows):
    return coded(2, 4, rows=rows) * 2 + coded(8, rows=rows) * 2 + [pltpu.SemaphoreType.DMA((16,))] * 2


def on_device(pre, dec, w, lw, sw, up, ow, rate, bias, skip, gain, start, at_position, slots, adapter):
    vmem = pl.BlockSpec(memory_space=pltpu.VMEM)
    smem = pl.BlockSpec(memory_space=pltpu.SMEM)
    any_ = pl.BlockSpec(memory_space=pltpu.HBM)
    dma = pltpu.SemaphoreType.DMA
    dec = dec.reshape(96, 256)
    sum_pre, sum_dec = pl.pallas_call(
        layer,
        out_shape=(jax.ShapeDtypeStruct((64, 256), F32), jax.ShapeDtypeStruct((96, 256), F32)),
        in_specs=[vmem, vmem, any_, vmem, vmem, vmem, any_, any_, vmem] + [smem] * 6,
        out_specs=(vmem, vmem),
        scratch_shapes=[
            pltpu.VMEM((16, 2, 256, 256), jnp.bfloat16),
            pltpu.VMEM((16, 2, 128, 256), jnp.bfloat16),
            pltpu.VMEM((2, 128, 128), F32),
            dma((33,)),
            dma((36,)),
            dma((36,)),
            pltpu.VMEM((2, 160, 256), jnp.bfloat16),
            pltpu.VMEM((2, 10, 16, 256), F32),
            pltpu.VMEM((10, 16, 256), F32),
            pltpu.VMEM((10, 16, 256), F32),
            dma((1,)),
            dma((1,)),
            *coded(10, rows=16),
            *coded(16, rows=16),
            dma((10,)),
            dma((16,)),
            *coded(10, 2, rows=16),
            dma((16,)),
            dma((10,)),
            dma((10,)),
            dma((10,)),
            pltpu.VMEM((8, 128, 128), F32),
            pltpu.VMEM((8, 96, 128), F32),
            pltpu.VMEM((8, 96, 128), F32),
            pltpu.VMEM((256, 128), F32),
            dma((2, 8)),
            dma((2, 8)),
            pltpu.VMEM((2, 64, 128), jnp.bfloat16),
            pltpu.VMEM((2, 96, 128), jnp.bfloat16),
            base_scratch(160),
            z_scratch(64),
            y_scratch(96),
            base_scratch(64),
            z_scratch(64),
            base_scratch(96),
            y_scratch(96),
        ],
        compiler_params=pltpu.CompilerParams(
            collective_id=0, has_side_effects=True, vmem_limit_bytes=60 * 1024 * 1024
        ),
        name="layer",
    )(
        pre, dec, w, lw, sw.T, up, ow, start.reshape(2, 128, 128), gain[None], rate, bias, skip,
        at_position, slots, adapter,
    )
    return pre.astype(F32) + sum_pre, (dec.astype(F32) + sum_dec).reshape(3, 32, 256)


def solution(mesh):
    placed = (
        P("grp", "head"),
        P(None, "grp", "head"),
        P("head", None),
        P("head", None),
        P("head", None),
        P(None, "head"),
        P("head", None),
        P("head"),
        P("head"),
        P("head"),
        P("head"),
        P("grp", "head", None, None),
        P(),
        P("grp"),
        P(),
    )
    return jax.shard_map(
        on_device,
        mesh=mesh,
        in_specs=placed,
        out_specs=(P("grp", "head"), P(None, "grp", "head")),
        check_vma=False,
    )
```

```python
import jax
import jax.numpy as jnp
from jax import lax
from jax.experimental import pallas as pl
from jax.experimental.pallas import tpu as pltpu
from jax.sharding import PartitionSpec as P

HI = lax.Precision.HIGHEST
F32 = jnp.float32
IN_BOUND = 3100.0
OUT_BOUND = 1500.0
START_BOUND = 18.1
TAIL_BOUND = 2.4e8


def iota(shape, dim):
    return lax.broadcasted_iota(jnp.int32, shape, dim)


def dot(a, b, dims=((1,), (0,)), precision=None):
    return lax.dot_general(a, b, (dims, ((), ())), precision=precision, preferred_element_type=F32)


def rem(a, n):
    return lax.rem(jnp.int32(a), jnp.int32(n))


def div(a, n):
    return lax.div(jnp.int32(a), jnp.int32(n))


def turn(i):
    return 4 + (1 - 2 * rem(i, 2)) * div(i + 1, 2)


def split(v):
    high = v.astype(jnp.bfloat16)
    return high, (v - high.astype(F32)).astype(jnp.bfloat16)


def channels(proj, low, tenant, head_at, up, rate, bias):
    rows = proj.shape[0]
    lane = iota((rows, 128), 1)
    picked = jnp.where(lane // 16 == tenant, low[:, 256:384], 0.0).astype(jnp.bfloat16)
    values = jnp.concatenate([proj[:, 0:64], proj[:, 128:192]], axis=1) + dot(picked, up)
    gate = jnp.concatenate([proj[:, 64:128], proj[:, 192:256]], axis=1)
    raw = low[:, 384:512]
    first = jnp.sum(jnp.where(lane == 2 * head_at, raw, 0.0), axis=1, keepdims=True)
    second = jnp.sum(jnp.where(lane == 2 * head_at + 1, raw, 0.0), axis=1, keepdims=True)
    raw = jnp.where(lane < 64, first, second) + bias
    length = jnp.maximum(raw, 0.0) + jnp.log1p(jnp.exp(-jnp.abs(raw)))
    return values, gate, length, -(length * rate)


def causal(rows):
    t, s = iota((rows, rows), 0), iota((rows, rows), 1)
    return (t >= s) & (t // 32 == s // 32)


def run(decay):
    return dot(causal(decay.shape[0]).astype(F32), decay, precision=HI)


def tail_values(values, length, running):
    parts, grown = [], []
    for i in range(2):
        at = slice(32 * i, 32 * i + 32)
        last = running[32 * i + 31 : 32 * i + 32]
        parts.append(jnp.exp(last - running[at]) * length[at] * values[at])
        grown.append(jnp.broadcast_to(jnp.exp(last), (8, 128)))
    return jnp.concatenate(parts, axis=0), jnp.concatenate(grown, axis=0)


def dot3(a, b, dims=((1,), (0,))):
    return dot(a[0], b[0], dims) + (dot(a[0], b[1], dims) + dot(a[1], b[0], dims))


def prefill(values, length, running, writer, reader, start, skip):
    rows = values.shape[0]
    keep = causal(rows)
    running_t, length_t = running.T, length.T
    scores = dot(reader, writer, ((1,), (1,)), HI)
    parts = []
    for h in range(2):
        spread = running[:, 64 * h : 64 * h + 1] - running_t[64 * h : 64 * h + 1, :]
        weight = jnp.where(keep, jnp.exp(jnp.where(keep, spread, 0.0)), 0.0)
        mixed = weight * length_t[64 * h : 64 * h + 1, :] * scores
        parts.append(dot(mixed, values, precision=HI))
    y = jnp.where(iota((rows, 128), 1) < 64, parts[0], parts[1]) + skip * values
    carried = [dot(reader[32 * i : 32 * i + 32], start[i], ((1,), (1,)), HI) for i in range(2)]
    return y + jnp.exp(running) * jnp.concatenate(carried, axis=0)


def decode(values, length, decay, writer, reader, skip):
    out, grown, total, totals = [], [], None, []
    for s in range(3):
        at = slice(32 * s, 32 * s + 32)
        total = decay[at] if total is None else total + decay[at]
        totals.append(total)
        grown.append(jnp.exp(total))
        y = skip * values[at]
        for u in range(s + 1):
            au = slice(32 * u, 32 * u + 32)
            score = jnp.sum(reader[at] * writer[au], axis=1, keepdims=True)
            term = length[au] * values[au] * score
            y = y + (term if u == s else jnp.exp(total - totals[u]) * term)
        out.append(y)
    return jnp.concatenate(out, axis=0), jnp.concatenate(grown, axis=0)


def normalise(y, gate, gain):
    gated = y * (gate * jax.nn.sigmoid(gate))
    scale = lax.rsqrt(jnp.mean(gated * gated, axis=1, keepdims=True) + 1e-5)
    return (gated * scale * gain).astype(jnp.bfloat16)


def encode(v, bound):
    a = jnp.abs(v) + 1e-30
    a = a * lax.rsqrt(a)
    a = a * lax.rsqrt(a)
    a = a * lax.rsqrt(a)
    a = a * (32767.0 / bound**0.125)
    return jnp.round(jnp.where(v < 0.0, -a, a)).astype(jnp.int32).astype(jnp.int16)


def plain(code, bound):
    a = code.astype(jnp.int32).astype(F32) * (bound**0.125 / 32767.0)
    b = a * a
    return a * jnp.abs(a) * b * (b * b)


class Copies:
    def __init__(self, out, into, source, target, sent, got, slot_sent, slot_got, device):
        self.all = [
            pltpu.make_async_remote_copy(
                src_ref=out.at[source],
                dst_ref=into.at[target],
                send_sem=sent.at[slot_sent],
                recv_sem=got.at[slot_got],
                device_id=device,
                device_id_type=pl.DeviceIdType.MESH,
            )
        ]

    def start(self):
        for copy in self.all:
            copy.start()

    def wait_recv(self):
        for copy in self.all:
            copy.wait_recv()

    def wait_send(self):
        for copy in self.all:
            copy.wait_send()


class Reduce:
    def __init__(self, place, part, lo, hi, bound, scratch):
        self.z, self.y, self.c = place
        self.part, self.lo, self.hi, self.bound = part, lo, hi, bound
        self.side, self.other, self.out, self.into, self.sent, self.got = scratch

    def block(self, zp, yp):
        return self.part[zp, yp, pl.ds(self.lo, self.hi - self.lo)]

    def pair(self, zp):
        return pltpu.make_async_remote_copy(
            src_ref=self.side.at[zp],
            dst_ref=self.other.at[zp],
            send_sem=self.sent.at[zp],
            recv_sem=self.got.at[zp],
            device_id={"head": self.z * 4 + (1 - self.y) * 2 + self.c},
            device_id_type=pl.DeviceIdType.MESH,
        )

    def far(self, zp, source):
        return pltpu.make_async_remote_copy(
            src_ref=self.out.at[zp],
            dst_ref=self.into.at[source],
            send_sem=self.sent.at[8 + zp],
            recv_sem=self.got.at[8 + source],
            device_id={"head": zp * 4 + self.y * 2 + self.c},
            device_id_type=pl.DeviceIdType.MESH,
        )

    def cross(self, i):
        zp = rem(self.z + turn(i), 8)
        self.side[zp] = encode(self.block(zp, 1 - self.y), self.bound)
        self.pair(zp).start()

    def paired(self, zp):
        total = self.block(zp, self.y)
        self.pair(zp).wait_recv()
        return total + plain(self.other[zp], self.bound)

    def direct(self, i):
        zp = rem(self.z + turn(i), 8)
        self.out[zp] = encode(self.paired(zp), self.bound)
        self.far(zp, self.z).start()

    def finish(self):
        total = self.paired(self.z)
        for j in (1, 7, 2, 6, 3, 5, 4):
            zp = rem(self.z + j, 8)
            self.far(zp, zp).wait_recv()
            total = total + plain(self.into[zp], self.bound)
        return total

    def drain(self):
        @pl.loop(0, 8)
        def _(j):
            self.pair(jnp.int32(j)).wait_send()

        @pl.loop(1, 8)
        def _(j):
            zp = rem(self.z + j, 8)
            self.far(zp, self.z).wait_send()


def layer(
    pre, dec, w_hbm, lw, swt, up, ow_hbm, start_hbm, gain, rates, biases, skips, at_position, slots, adapter,
    out_pre, out_dec,
    w, ow, start, load, w_sent, w_got, near, far, near_sent, near_got,
    rows, low_part, low_near, low_far, low_sent, low_got,
    owe, owed, owe_sent, owe_got,
    unit, unit_sent, unit_got, pass_sent, pass_got,
    starts, writers, tails, share_sent, share_got,
    begun, weight, norm_pre, norm_dec, base_in, in_pre, in_dec, base_pre, red_pre, base_dec, red_dec,
):
    group, head_at = lax.axis_index("grp"), lax.axis_index("head")
    z, y, c = div(head_at, 4), rem(div(head_at, 2), 2), rem(head_at, 2)
    chip = z * 2 + y
    place = (z, y, c)
    mesh_id = pl.DeviceIdType.MESH

    def columns(block, core):
        return pl.ds(pl.multiple_of((block * 2 + core) * 256, 256), 256)

    def w_own(zp):
        at = pl.ds(pl.multiple_of(zp * 1024, 1024), 1024)
        return pltpu.make_async_copy(w_hbm.at[:, at], w.at[zp], load.at[zp])

    def ow_own(b):
        return pltpu.make_async_copy(ow_hbm.at[:, columns(b, c)], ow.at[b, 0], load.at[16 + b])

    def to_core(source, target, slot):
        return pltpu.make_async_remote_copy(
            src_ref=source,
            dst_ref=target,
            send_sem=w_sent.at[slot],
            recv_sem=w_got.at[slot],
            device_id={"head": chip * 2 + 1 - c},
            device_id_type=mesh_id,
        )

    def near_copy(zp):
        return pltpu.make_async_remote_copy(
            src_ref=near.at[zp],
            dst_ref=far.at[zp],
            send_sem=near_sent.at[zp],
            recv_sem=near_got.at[zp],
            device_id={"head": chip * 2 + 1 - c},
            device_id_type=mesh_id,
        )

    def ow_other(b):
        return to_core(ow_hbm.at[:, columns(b, 1 - c)], ow.at[b, 1], 16 + b)

    normed_pre_other = to_core(norm_pre.at[0], norm_pre.at[1], 34)
    normed_dec_other = to_core(norm_dec.at[0], norm_dec.at[1], 35)

    @pl.loop(0, 8)
    def _(i):
        w_own(rem(z + turn(i), 8)).start()

    start_copy = pltpu.make_async_copy(start_hbm, start, load.at[32])
    start_copy.start()

    barrier = pltpu.get_barrier_semaphore()

    @pl.loop(1, 16)
    def _(j):
        pl.semaphore_signal(barrier, 1, device_id={"head": rem(chip + j, 16) * 2 + c}, device_id_type=mesh_id)

    @pl.loop(1, 8)
    def _(j):
        pl.semaphore_signal(barrier, 1, device_id={"grp": rem(group + j, 8)}, device_id_type=mesh_id)

    pl.semaphore_signal(barrier, 1, device_id={"head": chip * 2 + 1 - c}, device_id_type=mesh_id)

    @pl.loop(0, 16)
    def _(b):
        ow_own(b).start()

    rows[0:64] = pre[...]
    rows[64:160] = dec[...]
    part = dot(rows[...], lw[...])
    low_part[0] = part[:, 0:256].reshape(10, 16, 256)
    raw = dot(rows[...], swt[...], ((1,), (1,)))
    low_part[1] = jnp.concatenate([part[:, 256:384], raw, jnp.zeros_like(raw)], axis=1).reshape(10, 16, 256)
    low_near[...] = low_part[1 - c]

    spot = iota((64, 128), 0)
    prompt_pre = jnp.where(spot < 32, at_position[2 * group], at_position[2 * group + 1])
    spot = iota((32, 128), 0)
    prompt_dec = jnp.zeros((32, 128), jnp.int32)
    for j in range(32):
        prompt_dec = jnp.where(spot == j, div(slots[j], 16), prompt_dec)
    tenant_pre = jnp.zeros((64, 128), jnp.int32)
    tenant_dec = jnp.zeros((32, 128), jnp.int32)
    where_dec = jnp.full((32, 128), -1, jnp.int32)
    for j in range(16):
        tenant_pre = jnp.where(prompt_pre == j, adapter[j], tenant_pre)
        tenant_dec = jnp.where(prompt_dec == j, adapter[j], tenant_dec)
        where_dec = jnp.where(prompt_dec == at_position[j], j, where_dec)
    tenant_dec = jnp.concatenate([tenant_dec] * 3, axis=0)
    where_dec = jnp.concatenate([where_dec] * 3, axis=0)

    pl.semaphore_wait(barrier, 23)
    low_core = pltpu.make_async_remote_copy(
        src_ref=low_near,
        dst_ref=low_far,
        send_sem=low_sent.at[0],
        recv_sem=low_got.at[0],
        device_id={"head": chip * 2 + 1 - c},
        device_id_type=mesh_id,
    )
    low_core.start()

    def share(ref, kind, source, g):
        return pltpu.make_async_remote_copy(
            src_ref=ref.at[source],
            dst_ref=ref.at[source],
            send_sem=share_sent.at[kind, g],
            recv_sem=share_got.at[kind, source],
            device_id={"grp": g},
            device_id_type=mesh_id,
        )

    def to_groups(ref, kind):
        @pl.loop(1, 8)
        def _(j):
            share(ref, kind, group, rem(group + j, 8)).start()

    def from_groups(ref, kind):
        @pl.loop(1, 8)
        def _(j):
            g = rem(group + j, 8)
            share(ref, kind, g, g).wait_recv()

    def owe_copy(u, source):
        return Copies(
            owe, owed, u, source, owe_sent, owe_got, u, source, {"head": u * 2 + c}
        )

    def unit_copy(k, to):
        return Copies(
            unit, unit, (k, c), (k, c), unit_sent, unit_got, to, k, {"head": to * 2 + c}
        )

    def pass_copy(k, core):
        return Copies(
            unit, unit, (k, core), (k, core), pass_sent, pass_got, k, k,
            {"head": chip * 2 + 1 - c},
        )

    first_pre = Reduce(place, base_in, 0, 64, IN_BOUND, in_pre)
    first_dec = Reduce(place, base_in, 64, 160, IN_BOUND, in_dec)
    def piece(zp, yp, core):
        at = pl.ds(pl.multiple_of((yp * 2 + core) * 256, 256), 256)
        return dot(rows[...], w[zp, :, at])

    def give(i):
        zp = rem(z + turn(i), 8)
        w_own(zp).wait()
        for yp in range(2):
            near[zp, yp] = piece(zp, yp, 1 - c)
        near_copy(zp).start()

    def project(a, b):
        @pl.loop(a, b)
        def _(i):
            @pl.when(i < 6)
            def _():
                give(i + 2)

            zp = rem(z + turn(i), 8)
            own = [piece(zp, yp, c) for yp in range(2)]
            near_copy(zp).wait_recv()
            for yp in range(2):
                base_in[zp, yp] = own[yp] + far[zp, yp]
            first_pre.cross(i)

    @pl.loop(0, 2)
    def _(i):
        give(i)

    project(0, 3)
    low_core.wait_recv()

    @pl.loop(0, 10)
    def _(u):
        owe[u] = encode(low_part[c, u] + low_far[u], IN_BOUND)

        @pl.when(u != chip)
        def _():
            owe_copy(u, chip).start()

    project(3, 8)

    @pl.loop(0, 7)
    def _(i):
        first_dec.cross(i)
        first_pre.direct(i)

    first_dec.cross(7)
    start_copy.wait()
    for i in range(2):
        starts[group, 128 * i : 128 * i + 128] = encode(start[i], START_BOUND)
    to_groups(starts, 0)

    @pl.when(chip < 10)
    def _():
        owed[chip] = owe[chip]
        total = plain(owed[chip], IN_BOUND)
        for j in range(1, 16):
            source = rem(chip + j, 16)
            owe_copy(chip, source).wait_recv()
            total = total + plain(owed[source], IN_BOUND)
        unit[chip, c] = encode(total, IN_BOUND)

        @pl.loop(1, 16)
        def _(j):
            unit_copy(chip, rem(chip + j, 16)).start()

    @pl.loop(0, 7)
    def _(i):
        first_dec.direct(i)

    @pl.loop(0, 16)
    def _(b):
        ow_other(b).start()

    @pl.loop(0, 10)
    def _(k):
        @pl.when(k != chip)
        def _():
            unit_copy(k, chip).wait_recv()

        pass_copy(k, c).start()

    @pl.loop(0, 10)
    def _(k):
        pass_copy(k, 1 - c).wait_recv()

    lows = jnp.concatenate(
        [plain(unit[:, core], IN_BOUND).reshape(160, 256) for core in range(2)], axis=1
    )
    writers[group] = encode(lows[0:64, 0:128], IN_BOUND)
    to_groups(writers, 1)
    reader_high, reader_rest = split(lows[64:160, 128:256])

    half = iota((1, 128), 1) < 64
    rate = jnp.where(half, rates[0], rates[1])
    bias = jnp.where(half, biases[0], biases[1])
    skip = jnp.where(half, skips[0], skips[1])
    low_pre, low_dec = lows[0:64], lows[64:160]
    values, gate, length, decay = channels(first_pre.finish(), low_pre, tenant_pre, head_at, up[...], rate, bias)
    running = run(decay)
    carried, last = tail_values(values, length, running)
    tails[group, 0:64] = encode(carried, TAIL_BOUND)
    tails[group, 64:80] = encode(last, 1.0)
    to_groups(tails, 2)
    y_out = prefill(values, length, running, low_pre[:, 0:128], low_pre[:, 128:256], start, skip)
    norm_pre[0] = normalise(y_out, gate, gain[...])
    normed_pre_other.start()

    def spread(reduce, normed):
        both = jnp.concatenate([normed[0], normed[1]], axis=1)

        @pl.loop(0, 8)
        def _(i):
            zp = rem(z + turn(i), 8)
            for yp in range(2):
                reduce.part[zp, yp] = dot(both, ow[zp * 2 + yp].reshape(256, 256))
            reduce.cross(i)

    def forward(reduce):
        @pl.loop(0, 7)
        def _(i):
            reduce.direct(i)

    @pl.loop(0, 16)
    def _(b):
        ow_own(b).wait()
        ow_other(b).wait_recv()

    second = Reduce(place, base_pre, 0, 64, OUT_BOUND, red_pre)
    normed_pre_other.wait_recv()
    spread(second, norm_pre)
    values, gate, length, decay = channels(first_dec.finish(), low_dec, tenant_dec, head_at, up[...], rate, bias)
    from_groups(starts, 0)
    pick = jnp.zeros((96, 128), F32)
    for g in range(8):
        both = dot3((reader_high, reader_rest), split(plain(starts[g], START_BOUND)), ((1,), (1,)))
        pick = jnp.where(where_dec == 2 * g, both[:, 0:128], pick)
        pick = jnp.where(where_dec == 2 * g + 1, both[:, 128:256], pick)
    begun[...] = pick
    from_groups(writers, 1)
    scores = dot3(
        (reader_high, reader_rest), split(plain(writers[...], IN_BOUND).reshape(512, 128)), ((1,), (1,))
    )
    spot = jnp.concatenate([where_dec] * 4, axis=1)
    weight[...] = jnp.where(spot == iota((96, 512), 1) // 32, scores, 0.0)
    y_own, grown = decode(values, length, decay, low_dec[:, 0:128], low_dec[:, 128:256], skip)
    forward(second)

    from_groups(tails, 2)
    scaled = jnp.zeros((96, 128), F32)
    for i in range(16):
        grown_i = plain(tails[i // 2, 64:80], 1.0)[8 * (i % 2) : 8 * (i % 2) + 1]
        scaled = jnp.where(where_dec == i, grown_i, scaled)
    carried = plain(tails[:, 0:64], TAIL_BOUND).reshape(512, 128)
    seen = scaled * begun[...] + dot3(split(weight[...]), split(carried))
    norm_dec[0] = normalise(y_own + grown * seen, gate, gain[...])
    normed_dec_other.start()
    third = Reduce(place, base_dec, 0, 96, OUT_BOUND, red_dec)
    normed_dec_other.wait_recv()
    spread(third, norm_dec)
    forward(third)
    out_pre[...] = second.finish()
    out_dec[...] = third.finish()

    for reduce in (first_pre, first_dec, second, third):
        reduce.drain()
    for copy in (normed_pre_other, normed_dec_other):
        copy.wait_send()

    @pl.loop(0, 8)
    def _(i):
        near_copy(jnp.int32(i)).wait_send()

    @pl.loop(0, 16)
    def _(b):
        ow_other(b).wait_send()

    low_core.wait_send()

    @pl.loop(0, 10)
    def _(k):
        @pl.when(k != chip)
        def _():
            owe_copy(k, chip).wait_send()

        pass_copy(k, c).wait_send()

    @pl.when(chip < 10)
    def _():
        @pl.loop(1, 16)
        def _(j):
            unit_copy(chip, rem(chip + j, 16)).wait_send()

    @pl.loop(1, 8)
    def _(j):
        g = rem(group + j, 8)
        share(starts, 0, group, g).wait_send()
        share(writers, 1, group, g).wait_send()
        share(tails, 2, group, g).wait_send()


def coded(*lead, rows):
    return [pltpu.VMEM((*lead, rows, 256), jnp.int16)]


def base_scratch(rows):
    return pltpu.VMEM((8, 2, rows, 256), F32)


def reduce_scratch(rows):
    return coded(8, rows=rows) * 4 + [pltpu.SemaphoreType.DMA((16,))] * 2


def on_device(pre, dec, w, lw, sw, up, ow, rate, bias, skip, gain, start, at_position, slots, adapter):
    vmem = pl.BlockSpec(memory_space=pltpu.VMEM)
    smem = pl.BlockSpec(memory_space=pltpu.SMEM)
    any_ = pl.BlockSpec(memory_space=pltpu.HBM)
    dma = pltpu.SemaphoreType.DMA
    dec = dec.reshape(96, 256)
    sum_pre, sum_dec = pl.pallas_call(
        layer,
        out_shape=(jax.ShapeDtypeStruct((64, 256), F32), jax.ShapeDtypeStruct((96, 256), F32)),
        in_specs=[vmem, vmem, any_, vmem, vmem, vmem, any_, any_, vmem] + [smem] * 6,
        out_specs=(vmem, vmem),
        scratch_shapes=[
            pltpu.VMEM((8, 256, 1024), jnp.bfloat16),
            pltpu.VMEM((16, 2, 128, 256), jnp.bfloat16),
            pltpu.VMEM((2, 128, 128), F32),
            dma((33,)),
            dma((36,)),
            dma((36,)),
            pltpu.VMEM((8, 2, 160, 256), F32),
            pltpu.VMEM((8, 2, 160, 256), F32),
            dma((8,)),
            dma((8,)),
            pltpu.VMEM((160, 256), jnp.bfloat16),
            pltpu.VMEM((2, 10, 16, 256), F32),
            pltpu.VMEM((10, 16, 256), F32),
            pltpu.VMEM((10, 16, 256), F32),
            dma((1,)),
            dma((1,)),
            *coded(10, rows=16),
            *coded(16, rows=16),
            dma((10,)),
            dma((16,)),
            *coded(10, 2, rows=16),
            dma((16,)),
            dma((10,)),
            dma((10,)),
            dma((10,)),
            pltpu.VMEM((8, 256, 128), jnp.int16),
            pltpu.VMEM((8, 64, 128), jnp.int16),
            pltpu.VMEM((8, 80, 128), jnp.int16),
            dma((3, 8)),
            dma((3, 8)),
            pltpu.VMEM((96, 128), F32),
            pltpu.VMEM((96, 512), F32),
            pltpu.VMEM((2, 64, 128), jnp.bfloat16),
            pltpu.VMEM((2, 96, 128), jnp.bfloat16),
            base_scratch(160),
            reduce_scratch(64),
            reduce_scratch(96),
            base_scratch(64),
            reduce_scratch(64),
            base_scratch(96),
            reduce_scratch(96),
        ],
        compiler_params=pltpu.CompilerParams(
            collective_id=0, has_side_effects=True, vmem_limit_bytes=60 * 1024 * 1024
        ),
        name="layer",
    )(
        pre, dec, w, lw, sw.T, up, ow, start.reshape(2, 128, 128), gain[None], rate, bias, skip,
        at_position, slots, adapter,
    )
    return pre.astype(F32) + sum_pre, (dec.astype(F32) + sum_dec).reshape(3, 32, 256)


def solution(mesh):
    placed = (
        P("grp", "head"),
        P(None, "grp", "head"),
        P("head", None),
        P("head", None),
        P("head", None),
        P(None, "head"),
        P("head", None),
        P("head"),
        P("head"),
        P("head"),
        P("head"),
        P("grp", "head", None, None),
        P(),
        P("grp"),
        P(),
    )
    return jax.shard_map(
        on_device,
        mesh=mesh,
        in_specs=placed,
        out_specs=(P("grp", "head"), P(None, "grp", "head")),
        check_vma=False,
    )
```

```python
import jax
import jax.numpy as jnp
from jax import lax
from jax.experimental import pallas as pl
from jax.experimental.pallas import tpu as pltpu
from jax.sharding import PartitionSpec as P

HI = lax.Precision.HIGHEST
F32 = jnp.float32
IN_BOUND = 3100.0
OUT_BOUND = 1500.0
START_BOUND = 18.1
TAIL_BOUND = 2.4e8


def iota(shape, dim):
    return lax.broadcasted_iota(jnp.int32, shape, dim)


def dot(a, b, dims=((1,), (0,)), precision=None):
    return lax.dot_general(a, b, (dims, ((), ())), precision=precision, preferred_element_type=F32)


def rem(a, n):
    return lax.rem(jnp.int32(a), jnp.int32(n))


def div(a, n):
    return lax.div(jnp.int32(a), jnp.int32(n))


def turn(i):
    return 4 + (1 - 2 * rem(i, 2)) * div(i + 1, 2)


def split(v):
    high = v.astype(jnp.bfloat16)
    return high, (v - high.astype(F32)).astype(jnp.bfloat16)


def channels(proj, low, tenant, head_at, up, rate, bias):
    rows = proj.shape[0]
    lane = iota((rows, 128), 1)
    picked = jnp.where(lane // 16 == tenant, low[:, 256:384], 0.0).astype(jnp.bfloat16)
    values = jnp.concatenate([proj[:, 0:64], proj[:, 128:192]], axis=1) + dot(picked, up)
    gate = jnp.concatenate([proj[:, 64:128], proj[:, 192:256]], axis=1)
    raw = low[:, 384:512]
    first = jnp.sum(jnp.where(lane == 2 * head_at, raw, 0.0), axis=1, keepdims=True)
    second = jnp.sum(jnp.where(lane == 2 * head_at + 1, raw, 0.0), axis=1, keepdims=True)
    raw = jnp.where(lane < 64, first, second) + bias
    length = jnp.maximum(raw, 0.0) + jnp.log1p(jnp.exp(-jnp.abs(raw)))
    return values, gate, length, -(length * rate)


def causal(rows):
    t, s = iota((rows, rows), 0), iota((rows, rows), 1)
    return (t >= s) & (t // 32 == s // 32)


def run(decay):
    return dot(causal(decay.shape[0]).astype(F32), decay, precision=HI)


def tail_values(values, length, running):
    parts, grown = [], []
    for i in range(2):
        at = slice(32 * i, 32 * i + 32)
        last = running[32 * i + 31 : 32 * i + 32]
        parts.append(jnp.exp(last - running[at]) * length[at] * values[at])
        grown.append(jnp.broadcast_to(jnp.exp(last), (8, 128)))
    return jnp.concatenate(parts, axis=0), jnp.concatenate(grown, axis=0)


def dot3(a, b, dims=((1,), (0,))):
    return dot(a[0], b[0], dims) + (dot(a[0], b[1], dims) + dot(a[1], b[0], dims))


def prefill(values, length, running, writer, reader, start, skip):
    rows = values.shape[0]
    keep = causal(rows)
    running_t, length_t = running.T, length.T
    scores = dot(reader, writer, ((1,), (1,)), HI)
    parts = []
    for h in range(2):
        spread = running[:, 64 * h : 64 * h + 1] - running_t[64 * h : 64 * h + 1, :]
        weight = jnp.where(keep, jnp.exp(jnp.where(keep, spread, 0.0)), 0.0)
        mixed = weight * length_t[64 * h : 64 * h + 1, :] * scores
        parts.append(dot(mixed, values, precision=HI))
    y = jnp.where(iota((rows, 128), 1) < 64, parts[0], parts[1]) + skip * values
    carried = [dot(reader[32 * i : 32 * i + 32], start[i], ((1,), (1,)), HI) for i in range(2)]
    return y + jnp.exp(running) * jnp.concatenate(carried, axis=0)


def decode(values, length, decay, writer, reader, skip):
    out, grown, total, totals = [], [], None, []
    for s in range(3):
        at = slice(32 * s, 32 * s + 32)
        total = decay[at] if total is None else total + decay[at]
        totals.append(total)
        grown.append(jnp.exp(total))
        y = skip * values[at]
        for u in range(s + 1):
            au = slice(32 * u, 32 * u + 32)
            score = jnp.sum(reader[at] * writer[au], axis=1, keepdims=True)
            term = length[au] * values[au] * score
            y = y + (term if u == s else jnp.exp(total - totals[u]) * term)
        out.append(y)
    return jnp.concatenate(out, axis=0), jnp.concatenate(grown, axis=0)


def normalise(y, gate, gain):
    gated = y * (gate * jax.nn.sigmoid(gate))
    scale = lax.rsqrt(jnp.mean(gated * gated, axis=1, keepdims=True) + 1e-5)
    return (gated * scale * gain).astype(jnp.bfloat16)


def encode(v, bound):
    a = jnp.abs(v) + 1e-30
    a = a * lax.rsqrt(a)
    a = a * lax.rsqrt(a)
    a = a * lax.rsqrt(a)
    a = a * (32767.0 / bound**0.125)
    return jnp.round(jnp.where(v < 0.0, -a, a)).astype(jnp.int32).astype(jnp.int16)


def plain(code, bound):
    a = code.astype(jnp.int32).astype(F32) * (bound**0.125 / 32767.0)
    b = a * a
    return a * jnp.abs(a) * b * (b * b)


class Copies:
    def __init__(self, out, into, source, target, sent, got, slot_sent, slot_got, device):
        self.all = [
            pltpu.make_async_remote_copy(
                src_ref=out.at[source],
                dst_ref=into.at[target],
                send_sem=sent.at[slot_sent],
                recv_sem=got.at[slot_got],
                device_id=device,
                device_id_type=pl.DeviceIdType.MESH,
            )
        ]

    def start(self):
        for copy in self.all:
            copy.start()

    def wait_recv(self):
        for copy in self.all:
            copy.wait_recv()

    def wait_send(self):
        for copy in self.all:
            copy.wait_send()


class Reduce:
    def __init__(self, place, part, lo, hi, bound, scratch):
        self.z, self.y, self.c = place
        self.part, self.lo, self.hi, self.bound = part, lo, hi, bound
        self.side, self.other, self.out, self.into, self.sent, self.got = scratch

    def block(self, zp, yp):
        return self.part[zp, yp, pl.ds(self.lo, self.hi - self.lo)]

    def pair(self, zp):
        return pltpu.make_async_remote_copy(
            src_ref=self.side.at[zp],
            dst_ref=self.other.at[zp],
            send_sem=self.sent.at[zp],
            recv_sem=self.got.at[zp],
            device_id={"head": self.z * 4 + (1 - self.y) * 2 + self.c},
            device_id_type=pl.DeviceIdType.MESH,
        )

    def far(self, zp, source):
        return pltpu.make_async_remote_copy(
            src_ref=self.out.at[zp],
            dst_ref=self.into.at[source],
            send_sem=self.sent.at[8 + zp],
            recv_sem=self.got.at[8 + source],
            device_id={"head": zp * 4 + self.y * 2 + self.c},
            device_id_type=pl.DeviceIdType.MESH,
        )

    def cross(self, i):
        zp = rem(self.z + turn(i), 8)
        self.side[zp] = encode(self.block(zp, 1 - self.y), self.bound)
        self.pair(zp).start()

    def paired(self, zp):
        total = self.block(zp, self.y)
        self.pair(zp).wait_recv()
        return total + plain(self.other[zp], self.bound)

    def direct(self, i):
        zp = rem(self.z + turn(i), 8)
        self.out[zp] = encode(self.paired(zp), self.bound)
        self.far(zp, self.z).start()

    def finish(self):
        total = self.paired(self.z)
        for j in (1, 7, 2, 6, 3, 5, 4):
            zp = rem(self.z + j, 8)
            self.far(zp, zp).wait_recv()
            total = total + plain(self.into[zp], self.bound)
        return total

    def drain(self):
        @pl.loop(0, 8)
        def _(j):
            self.pair(jnp.int32(j)).wait_send()

        @pl.loop(1, 8)
        def _(j):
            zp = rem(self.z + j, 8)
            self.far(zp, self.z).wait_send()


class Base:
    def __init__(self, place, scratch, fill, before=None):
        self.z, self.y, self.c = place
        self.near, self.far, self.part, self.sent, self.got = scratch
        self.fill, self.before = fill, before
        self.ready = set()

    def core_copy(self, zp):
        return pltpu.make_async_remote_copy(
            src_ref=self.near.at[zp],
            dst_ref=self.far.at[zp],
            send_sem=self.sent.at[zp],
            recv_sem=self.got.at[zp],
            device_id={"head": self.z * 4 + self.y * 2 + 1 - self.c},
            device_id_type=pl.DeviceIdType.MESH,
        )

    def spot(self, i):
        return rem(self.z + turn(i), 8)

    def near_of(self, a, b):
        @pl.loop(a, b)
        def _(i):
            zp = self.spot(i)
            if self.before is not None:
                self.before(zp)
            for yp in range(2):
                self.fill(self.near.at[zp, yp], zp, yp, 1 - self.c)
            self.core_copy(zp).start()

    def own_of(self, a, b):
        @pl.loop(a, b)
        def _(i):
            zp = self.spot(i)
            for yp in range(2):
                self.fill(self.part.at[zp, yp], zp, yp, self.c)

    def need(self, offset):
        zp = rem(self.z + offset, 8)
        if offset not in self.ready:
            self.ready.add(offset)
            self.core_copy(zp).wait_recv()
        return zp

    def drain(self):
        @pl.loop(0, 8)
        def _(i):
            self.core_copy(jnp.int32(i)).wait_send()


class Order:
    def __init__(self, base, lo, hi, bound, scratch):
        self.base, self.lo, self.hi, self.bound = base, lo, hi, bound
        self.z, self.y, self.c = base.z, base.y, base.c
        self.out, self.into, self.side, self.other, self.sent, self.got = scratch
        self.copies = []

    def block(self, zp, yp):
        at = (zp, yp, pl.ds(self.lo, self.hi - self.lo))
        return self.base.part[at] + self.base.far[at]

    def hop(self, at, slot, step):
        return Copies(
            self.out, self.into, at, at, self.sent, self.got, slot, slot,
            {"head": rem(self.z + step, 8) * 4 + self.y * 2 + self.c},
        )

    def pair(self, at, slot):
        return Copies(
            self.side, self.other, at, at, self.sent, self.got, slot, slot,
            {"head": self.z * 4 + (1 - self.y) * 2 + self.c},
        )

    def put(self, ref, at, v):
        ref[at] = encode(v, self.bound)

    def get(self, ref, at):
        return plain(ref[at], self.bound)

    def go(self, copy):
        copy.start()
        self.copies.append(copy)

    def drain(self):
        for copy in self.copies:
            copy.wait_send()


class ZFirst(Order):
    def message(self, side, yp, at):
        return self.hop((side, yp, at), side * 8 + yp * 4 + at, 1 if side else 7)

    def ring(self, t):
        for side in range(2):
            for yp in range(2):
                first = 4 if side == yp else 3
                away = first - t
                if away < 1:
                    continue
                total = self.block(self.base.need((away if side else 8 - away) % 8), yp)
                if away < first:
                    self.message(side, yp, away).wait_recv()
                    total = total + self.get(self.into, (side, yp, away))
                self.put(self.out, (side, yp, away - 1), total)
                self.go(self.message(side, yp, away - 1))

    def gathered(self, yp):
        return self.block(self.z, yp) + self.get(self.into, (0, yp, 0)) + self.get(self.into, (1, yp, 0))

    def across(self):
        self.base.need(0)
        for side in range(2):
            for yp in range(2):
                self.message(side, yp, 0).wait_recv()
        self.put(self.side, 0, self.gathered(1 - self.y))
        self.go(self.pair(0, 16))

    def finish(self):
        total = self.gathered(self.y)
        self.pair(0, 16).wait_recv()
        return total + self.get(self.other, 0)


class YFirst(Order):
    def cross(self, *offsets):
        for offset in offsets:
            zp = self.base.need(offset)
            self.put(self.side, zp, self.block(zp, 1 - self.y))
            self.go(self.pair(zp, 8 + zp))

    def message(self, side, at):
        return self.hop((side, at), side * 4 + at, 1 if side else 7)

    def paired(self, offset):
        zp = rem(self.z + offset, 8)
        total = self.block(zp, self.y)
        self.pair(zp, 8 + zp).wait_recv()
        return total + self.get(self.other, zp)

    def ring(self, t):
        for side in range(2):
            first = 3 if side else 4
            away = first - t
            if away < 1:
                continue
            total = self.paired((away if side else 8 - away) % 8)
            if away < first:
                self.message(side, away).wait_recv()
                total = total + self.get(self.into, (side, away))
            self.put(self.out, (side, away - 1), total)
            self.go(self.message(side, away - 1))

    def finish(self):
        total = self.paired(0)
        for side in range(2):
            self.message(side, 0).wait_recv()
        return total + self.get(self.into, (0, 0)) + self.get(self.into, (1, 0))


def layer(
    pre, dec, w_hbm, lw, swt, up, ow_hbm, start_hbm, gain, rates, biases, skips, at_position, slots, adapter,
    out_pre, out_dec,
    w, ow, start, load, w_sent, w_got, near, far, near_sent, near_got,
    rows, low_part, low_near, low_far, low_sent, low_got,
    owe, owed, owe_sent, owe_got,
    unit, unit_sent, unit_got, pass_sent, pass_got,
    starts, writers, tails, share_sent, share_got,
    begun, weight, norm_pre, norm_dec, base_in, in_pre, in_dec, base_pre, red_pre, base_dec, red_dec,
):
    group, head_at = lax.axis_index("grp"), lax.axis_index("head")
    z, y, c = div(head_at, 4), rem(div(head_at, 2), 2), rem(head_at, 2)
    chip = z * 2 + y
    place = (z, y, c)
    mesh_id = pl.DeviceIdType.MESH

    def columns(block, core):
        return pl.ds(pl.multiple_of((block * 2 + core) * 256, 256), 256)

    def w_own(zp):
        at = pl.ds(pl.multiple_of(zp * 1024, 1024), 1024)
        return pltpu.make_async_copy(w_hbm.at[:, at], w.at[zp], load.at[zp])

    def ow_own(b):
        return pltpu.make_async_copy(ow_hbm.at[:, columns(b, c)], ow.at[b, 0], load.at[16 + b])

    def to_core(source, target, slot):
        return pltpu.make_async_remote_copy(
            src_ref=source,
            dst_ref=target,
            send_sem=w_sent.at[slot],
            recv_sem=w_got.at[slot],
            device_id={"head": chip * 2 + 1 - c},
            device_id_type=mesh_id,
        )

    def ow_other(b):
        return to_core(ow_hbm.at[:, columns(b, 1 - c)], ow.at[b, 1], 16 + b)

    normed_pre_other = to_core(norm_pre.at[0], norm_pre.at[1], 34)
    normed_dec_other = to_core(norm_dec.at[0], norm_dec.at[1], 35)

    @pl.loop(0, 8)
    def _(i):
        w_own(rem(z + turn(i), 8)).start()

    start_copy = pltpu.make_async_copy(start_hbm, start, load.at[32])
    start_copy.start()

    barrier = pltpu.get_barrier_semaphore()

    @pl.loop(1, 16)
    def _(j):
        pl.semaphore_signal(barrier, 1, device_id={"head": rem(chip + j, 16) * 2 + c}, device_id_type=mesh_id)

    @pl.loop(1, 8)
    def _(j):
        pl.semaphore_signal(barrier, 1, device_id={"grp": rem(group + j, 8)}, device_id_type=mesh_id)

    pl.semaphore_signal(barrier, 1, device_id={"head": chip * 2 + 1 - c}, device_id_type=mesh_id)

    @pl.loop(0, 16)
    def _(b):
        ow_own(b).start()

    rows[0:64] = pre[...]
    rows[64:160] = dec[...]
    part = dot(rows[...], lw[...])
    low_part[0] = part[:, 0:256].reshape(10, 16, 256)
    raw = dot(rows[...], swt[...], ((1,), (1,)))
    low_part[1] = jnp.concatenate([part[:, 256:384], raw, jnp.zeros_like(raw)], axis=1).reshape(10, 16, 256)
    low_near[...] = low_part[1 - c]

    spot = iota((64, 128), 0)
    prompt_pre = jnp.where(spot < 32, at_position[2 * group], at_position[2 * group + 1])
    spot = iota((32, 128), 0)
    prompt_dec = jnp.zeros((32, 128), jnp.int32)
    for j in range(32):
        prompt_dec = jnp.where(spot == j, div(slots[j], 16), prompt_dec)
    tenant_pre = jnp.zeros((64, 128), jnp.int32)
    tenant_dec = jnp.zeros((32, 128), jnp.int32)
    where_dec = jnp.full((32, 128), -1, jnp.int32)
    for j in range(16):
        tenant_pre = jnp.where(prompt_pre == j, adapter[j], tenant_pre)
        tenant_dec = jnp.where(prompt_dec == j, adapter[j], tenant_dec)
        where_dec = jnp.where(prompt_dec == at_position[j], j, where_dec)
    tenant_dec = jnp.concatenate([tenant_dec] * 3, axis=0)
    where_dec = jnp.concatenate([where_dec] * 3, axis=0)

    pl.semaphore_wait(barrier, 23)
    low_core = pltpu.make_async_remote_copy(
        src_ref=low_near,
        dst_ref=low_far,
        send_sem=low_sent.at[0],
        recv_sem=low_got.at[0],
        device_id={"head": chip * 2 + 1 - c},
        device_id_type=mesh_id,
    )
    low_core.start()

    def share(ref, kind, source, g):
        return pltpu.make_async_remote_copy(
            src_ref=ref.at[source],
            dst_ref=ref.at[source],
            send_sem=share_sent.at[kind, g],
            recv_sem=share_got.at[kind, source],
            device_id={"grp": g},
            device_id_type=mesh_id,
        )

    def to_groups(ref, kind):
        @pl.loop(1, 8)
        def _(j):
            share(ref, kind, group, rem(group + j, 8)).start()

    def from_groups(ref, kind):
        @pl.loop(1, 8)
        def _(j):
            g = rem(group + j, 8)
            share(ref, kind, g, g).wait_recv()

    def owe_copy(u, source):
        return Copies(
            owe, owed, u, source, owe_sent, owe_got, u, source, {"head": u * 2 + c}
        )

    def unit_copy(k, to):
        return Copies(
            unit, unit, (k, c), (k, c), unit_sent, unit_got, to, k, {"head": to * 2 + c}
        )

    def pass_copy(k, core):
        return Copies(
            unit, unit, (k, core), (k, core), pass_sent, pass_got, k, k,
            {"head": chip * 2 + 1 - c},
        )

    def piece(zp, yp, core):
        at = pl.ds(pl.multiple_of((yp * 2 + core) * 256, 256), 256)
        return dot(rows[...], w[zp, :, at])

    def fill(ref, zp, yp, core):
        ref[...] = piece(zp, yp, core)

    base = Base(place, (near, far, base_in, near_sent, near_got), fill, lambda zp: w_own(zp).wait())
    zs, ys = ZFirst(base, 0, 64, IN_BOUND, in_pre), YFirst(base, 64, 160, IN_BOUND, in_dec)
    base.near_of(0, 3)
    low_core.wait_recv()

    @pl.loop(0, 10)
    def _(u):
        owe[u] = encode(low_part[c, u] + low_far[u], IN_BOUND)

        @pl.when(u != chip)
        def _():
            owe_copy(u, chip).start()

    base.near_of(3, 5)
    base.own_of(0, 3)
    zs.ring(0)
    ys.cross(4, 3)
    base.near_of(5, 8)
    base.own_of(3, 5)
    ys.cross(5, 2)
    ys.ring(0)

    @pl.when(chip < 10)
    def _():
        owed[chip] = owe[chip]
        total = plain(owed[chip], IN_BOUND)
        for j in range(1, 16):
            source = rem(chip + j, 16)
            owe_copy(chip, source).wait_recv()
            total = total + plain(owed[source], IN_BOUND)
        unit[chip, c] = encode(total, IN_BOUND)

        @pl.loop(1, 16)
        def _(j):
            unit_copy(chip, rem(chip + j, 16)).start()

    zs.ring(1)
    base.own_of(5, 8)
    ys.cross(6, 1)
    ys.ring(1)
    ys.cross(7, 0)
    start_copy.wait()
    for i in range(2):
        starts[group, 128 * i : 128 * i + 128] = encode(start[i], START_BOUND)
    to_groups(starts, 0)

    @pl.loop(0, 16)
    def _(b):
        ow_other(b).start()

    zs.ring(2)

    @pl.loop(0, 10)
    def _(k):
        @pl.when(k != chip)
        def _():
            unit_copy(k, chip).wait_recv()

        pass_copy(k, c).start()

    ys.ring(2)
    zs.ring(3)
    ys.ring(3)
    zs.across()

    @pl.loop(0, 10)
    def _(k):
        pass_copy(k, 1 - c).wait_recv()

    lows = jnp.concatenate(
        [plain(unit[:, core], IN_BOUND).reshape(160, 256) for core in range(2)], axis=1
    )
    writers[group] = encode(lows[0:64, 0:128], IN_BOUND)
    to_groups(writers, 1)
    reader_high, reader_rest = split(lows[64:160, 128:256])

    half = iota((1, 128), 1) < 64
    rate = jnp.where(half, rates[0], rates[1])
    bias = jnp.where(half, biases[0], biases[1])
    skip = jnp.where(half, skips[0], skips[1])
    low_pre, low_dec = lows[0:64], lows[64:160]
    values, gate, length, decay = channels(zs.finish(), low_pre, tenant_pre, head_at, up[...], rate, bias)
    running = run(decay)
    carried, last = tail_values(values, length, running)
    tails[group, 0:64] = encode(carried, TAIL_BOUND)
    tails[group, 64:80] = encode(last, 1.0)
    to_groups(tails, 2)
    y_out = prefill(values, length, running, low_pre[:, 0:128], low_pre[:, 128:256], start, skip)
    norm_pre[0] = normalise(y_out, gate, gain[...])
    normed_pre_other.start()

    def spread(reduce, normed):
        both = jnp.concatenate([normed[0], normed[1]], axis=1)

        @pl.loop(0, 8)
        def _(i):
            zp = rem(z + turn(i), 8)
            for yp in range(2):
                reduce.part[zp, yp] = dot(both, ow[zp * 2 + yp].reshape(256, 256))
            reduce.cross(i)

    def forward(reduce):
        @pl.loop(0, 7)
        def _(i):
            reduce.direct(i)

    @pl.loop(0, 16)
    def _(b):
        ow_own(b).wait()
        ow_other(b).wait_recv()

    second = Reduce(place, base_pre, 0, 64, OUT_BOUND, red_pre)
    normed_pre_other.wait_recv()
    spread(second, norm_pre)
    values, gate, length, decay = channels(ys.finish(), low_dec, tenant_dec, head_at, up[...], rate, bias)
    from_groups(starts, 0)
    pick = jnp.zeros((96, 128), F32)
    for g in range(8):
        both = dot3((reader_high, reader_rest), split(plain(starts[g], START_BOUND)), ((1,), (1,)))
        pick = jnp.where(where_dec == 2 * g, both[:, 0:128], pick)
        pick = jnp.where(where_dec == 2 * g + 1, both[:, 128:256], pick)
    begun[...] = pick
    from_groups(writers, 1)
    scores = dot3(
        (reader_high, reader_rest), split(plain(writers[...], IN_BOUND).reshape(512, 128)), ((1,), (1,))
    )
    spot = jnp.concatenate([where_dec] * 4, axis=1)
    weight[...] = jnp.where(spot == iota((96, 512), 1) // 32, scores, 0.0)
    y_own, grown = decode(values, length, decay, low_dec[:, 0:128], low_dec[:, 128:256], skip)

    forward(second)
    from_groups(tails, 2)
    scaled = jnp.zeros((96, 128), F32)
    for i in range(16):
        grown_i = plain(tails[i // 2, 64:80], 1.0)[8 * (i % 2) : 8 * (i % 2) + 1]
        scaled = jnp.where(where_dec == i, grown_i, scaled)
    carried = plain(tails[:, 0:64], TAIL_BOUND).reshape(512, 128)
    seen = scaled * begun[...] + dot3(split(weight[...]), split(carried))
    norm_dec[0] = normalise(y_own + grown * seen, gate, gain[...])
    normed_dec_other.start()
    third = Reduce(place, base_dec, 0, 96, OUT_BOUND, red_dec)
    normed_dec_other.wait_recv()
    spread(third, norm_dec)
    forward(third)
    out_pre[...] = second.finish()
    out_dec[...] = third.finish()

    for reduce in (base, zs, ys, second, third):
        reduce.drain()
    for copy in (normed_pre_other, normed_dec_other):
        copy.wait_send()

    @pl.loop(0, 16)
    def _(b):
        ow_other(b).wait_send()

    low_core.wait_send()

    @pl.loop(0, 10)
    def _(k):
        @pl.when(k != chip)
        def _():
            owe_copy(k, chip).wait_send()

        pass_copy(k, c).wait_send()

    @pl.when(chip < 10)
    def _():
        @pl.loop(1, 16)
        def _(j):
            unit_copy(chip, rem(chip + j, 16)).wait_send()

    @pl.loop(1, 8)
    def _(j):
        g = rem(group + j, 8)
        share(starts, 0, group, g).wait_send()
        share(writers, 1, group, g).wait_send()
        share(tails, 2, group, g).wait_send()


def coded(*lead, rows):
    return [pltpu.VMEM((*lead, rows, 256), jnp.int16)]


def base_scratch(rows):
    return pltpu.VMEM((8, 2, rows, 256), F32)


def z_scratch(rows):
    return coded(2, 2, 4, rows=rows) * 2 + coded(1, rows=rows) * 2 + [pltpu.SemaphoreType.DMA((17,))] * 2


def y_scratch(rows):
    return coded(2, 4, rows=rows) * 2 + coded(8, rows=rows) * 2 + [pltpu.SemaphoreType.DMA((16,))] * 2


def reduce_scratch(rows):
    return coded(8, rows=rows) * 4 + [pltpu.SemaphoreType.DMA((16,))] * 2


def on_device(pre, dec, w, lw, sw, up, ow, rate, bias, skip, gain, start, at_position, slots, adapter):
    vmem = pl.BlockSpec(memory_space=pltpu.VMEM)
    smem = pl.BlockSpec(memory_space=pltpu.SMEM)
    any_ = pl.BlockSpec(memory_space=pltpu.HBM)
    dma = pltpu.SemaphoreType.DMA
    dec = dec.reshape(96, 256)
    sum_pre, sum_dec = pl.pallas_call(
        layer,
        out_shape=(jax.ShapeDtypeStruct((64, 256), F32), jax.ShapeDtypeStruct((96, 256), F32)),
        in_specs=[vmem, vmem, any_, vmem, vmem, vmem, any_, any_, vmem] + [smem] * 6,
        out_specs=(vmem, vmem),
        scratch_shapes=[
            pltpu.VMEM((8, 256, 1024), jnp.bfloat16),
            pltpu.VMEM((16, 2, 128, 256), jnp.bfloat16),
            pltpu.VMEM((2, 128, 128), F32),
            dma((33,)),
            dma((36,)),
            dma((36,)),
            pltpu.VMEM((8, 2, 160, 256), F32),
            pltpu.VMEM((8, 2, 160, 256), F32),
            dma((8,)),
            dma((8,)),
            pltpu.VMEM((160, 256), jnp.bfloat16),
            pltpu.VMEM((2, 10, 16, 256), F32),
            pltpu.VMEM((10, 16, 256), F32),
            pltpu.VMEM((10, 16, 256), F32),
            dma((1,)),
            dma((1,)),
            *coded(10, rows=16),
            *coded(16, rows=16),
            dma((10,)),
            dma((16,)),
            *coded(10, 2, rows=16),
            dma((16,)),
            dma((10,)),
            dma((10,)),
            dma((10,)),
            pltpu.VMEM((8, 256, 128), jnp.int16),
            pltpu.VMEM((8, 64, 128), jnp.int16),
            pltpu.VMEM((8, 80, 128), jnp.int16),
            dma((3, 8)),
            dma((3, 8)),
            pltpu.VMEM((96, 128), F32),
            pltpu.VMEM((96, 512), F32),
            pltpu.VMEM((2, 64, 128), jnp.bfloat16),
            pltpu.VMEM((2, 96, 128), jnp.bfloat16),
            base_scratch(160),
            z_scratch(64),
            y_scratch(96),
            base_scratch(64),
            reduce_scratch(64),
            base_scratch(96),
            reduce_scratch(96),
        ],
        compiler_params=pltpu.CompilerParams(
            collective_id=0, has_side_effects=True, vmem_limit_bytes=60 * 1024 * 1024
        ),
        name="layer",
    )(
        pre, dec, w, lw, sw.T, up, ow, start.reshape(2, 128, 128), gain[None], rate, bias, skip,
        at_position, slots, adapter,
    )
    return pre.astype(F32) + sum_pre, (dec.astype(F32) + sum_dec).reshape(3, 32, 256)


def solution(mesh):
    placed = (
        P("grp", "head"),
        P(None, "grp", "head"),
        P("head", None),
        P("head", None),
        P("head", None),
        P(None, "head"),
        P("head", None),
        P("head"),
        P("head"),
        P("head"),
        P("head"),
        P("grp", "head", None, None),
        P(),
        P("grp"),
        P(),
    )
    return jax.shard_map(
        on_device,
        mesh=mesh,
        in_specs=placed,
        out_specs=(P("grp", "head"), P(None, "grp", "head")),
        check_vma=False,
    )
```

```python
import jax
import jax.numpy as jnp
from jax import lax
from jax.experimental import pallas as pl
from jax.experimental.pallas import tpu as pltpu
from jax.sharding import PartitionSpec as P

HI = lax.Precision.HIGHEST
F32 = jnp.float32
IN_BOUND = 3100.0
OUT_BOUND = 1500.0
START_BOUND = 18.1
TAIL_BOUND = 2.4e8


def iota(shape, dim):
    return lax.broadcasted_iota(jnp.int32, shape, dim)


def dot(a, b, dims=((1,), (0,)), precision=None):
    return lax.dot_general(a, b, (dims, ((), ())), precision=precision, preferred_element_type=F32)


def rem(a, n):
    return lax.rem(jnp.int32(a), jnp.int32(n))


def div(a, n):
    return lax.div(jnp.int32(a), jnp.int32(n))


def turn(i):
    return 4 + (1 - 2 * rem(i, 2)) * div(i + 1, 2)


def split(v):
    high = v.astype(jnp.bfloat16)
    return high, (v - high.astype(F32)).astype(jnp.bfloat16)


def channels(proj, low, tenant, head_at, up, rate, bias):
    rows = proj.shape[0]
    lane = iota((rows, 128), 1)
    picked = jnp.where(lane // 16 == tenant, low[:, 256:384], 0.0).astype(jnp.bfloat16)
    values = jnp.concatenate([proj[:, 0:64], proj[:, 128:192]], axis=1) + dot(picked, up)
    gate = jnp.concatenate([proj[:, 64:128], proj[:, 192:256]], axis=1)
    raw = low[:, 384:512]
    first = jnp.sum(jnp.where(lane == 2 * head_at, raw, 0.0), axis=1, keepdims=True)
    second = jnp.sum(jnp.where(lane == 2 * head_at + 1, raw, 0.0), axis=1, keepdims=True)
    raw = jnp.where(lane < 64, first, second) + bias
    length = jnp.maximum(raw, 0.0) + jnp.log1p(jnp.exp(-jnp.abs(raw)))
    return values, gate, length, -(length * rate)


def causal(rows):
    t, s = iota((rows, rows), 0), iota((rows, rows), 1)
    return (t >= s) & (t // 32 == s // 32)


def run(decay):
    return dot(causal(decay.shape[0]).astype(F32), decay, precision=HI)


def tail_values(values, length, running):
    parts, grown = [], []
    for i in range(2):
        at = slice(32 * i, 32 * i + 32)
        last = running[32 * i + 31 : 32 * i + 32]
        parts.append(jnp.exp(last - running[at]) * length[at] * values[at])
        grown.append(jnp.broadcast_to(jnp.exp(last), (8, 128)))
    return jnp.concatenate(parts, axis=0), jnp.concatenate(grown, axis=0)


def dot3(a, b, dims=((1,), (0,))):
    return dot(a[0], b[0], dims) + (dot(a[0], b[1], dims) + dot(a[1], b[0], dims))


def prefill(values, length, running, writer, reader, start, skip):
    rows = values.shape[0]
    keep = causal(rows)
    running_t, length_t = running.T, length.T
    scores = dot(reader, writer, ((1,), (1,)), HI)
    parts = []
    for h in range(2):
        spread = running[:, 64 * h : 64 * h + 1] - running_t[64 * h : 64 * h + 1, :]
        weight = jnp.where(keep, jnp.exp(jnp.where(keep, spread, 0.0)), 0.0)
        mixed = weight * length_t[64 * h : 64 * h + 1, :] * scores
        parts.append(dot(mixed, values, precision=HI))
    y = jnp.where(iota((rows, 128), 1) < 64, parts[0], parts[1]) + skip * values
    carried = [dot(reader[32 * i : 32 * i + 32], start[i], ((1,), (1,)), HI) for i in range(2)]
    return y + jnp.exp(running) * jnp.concatenate(carried, axis=0)


def decode(values, length, decay, writer, reader, skip):
    out, grown, total, totals = [], [], None, []
    for s in range(3):
        at = slice(32 * s, 32 * s + 32)
        total = decay[at] if total is None else total + decay[at]
        totals.append(total)
        grown.append(jnp.exp(total))
        y = skip * values[at]
        for u in range(s + 1):
            au = slice(32 * u, 32 * u + 32)
            score = jnp.sum(reader[at] * writer[au], axis=1, keepdims=True)
            term = length[au] * values[au] * score
            y = y + (term if u == s else jnp.exp(total - totals[u]) * term)
        out.append(y)
    return jnp.concatenate(out, axis=0), jnp.concatenate(grown, axis=0)


def normalise(y, gate, gain):
    gated = y * (gate * jax.nn.sigmoid(gate))
    scale = lax.rsqrt(jnp.mean(gated * gated, axis=1, keepdims=True) + 1e-5)
    return (gated * scale * gain).astype(jnp.bfloat16)


def encode(v, bound):
    a = jnp.abs(v) + 1e-30
    a = a * lax.rsqrt(a)
    a = a * lax.rsqrt(a)
    a = a * lax.rsqrt(a)
    a = a * (32767.0 / bound**0.125)
    return jnp.round(jnp.where(v < 0.0, -a, a)).astype(jnp.int32).astype(jnp.int16)


def plain(code, bound):
    a = code.astype(jnp.int32).astype(F32) * (bound**0.125 / 32767.0)
    b = a * a
    return a * jnp.abs(a) * b * (b * b)


class Copies:
    def __init__(self, out, into, source, target, sent, got, slot_sent, slot_got, device):
        self.all = [
            pltpu.make_async_remote_copy(
                src_ref=out.at[source],
                dst_ref=into.at[target],
                send_sem=sent.at[slot_sent],
                recv_sem=got.at[slot_got],
                device_id=device,
                device_id_type=pl.DeviceIdType.MESH,
            )
        ]

    def start(self):
        for copy in self.all:
            copy.start()

    def wait_recv(self):
        for copy in self.all:
            copy.wait_recv()

    def wait_send(self):
        for copy in self.all:
            copy.wait_send()


class Reduce:
    def __init__(self, place, part, lo, hi, bound, scratch):
        self.z, self.y, self.c = place
        self.part, self.lo, self.hi, self.bound = part, lo, hi, bound
        self.side, self.other, self.out, self.into, self.sent, self.got = scratch

    def block(self, zp, yp):
        return self.part[zp, yp, pl.ds(self.lo, self.hi - self.lo)]

    def pair(self, zp):
        return pltpu.make_async_remote_copy(
            src_ref=self.side.at[zp],
            dst_ref=self.other.at[zp],
            send_sem=self.sent.at[zp],
            recv_sem=self.got.at[zp],
            device_id={"head": self.z * 4 + (1 - self.y) * 2 + self.c},
            device_id_type=pl.DeviceIdType.MESH,
        )

    def far(self, zp, source):
        return pltpu.make_async_remote_copy(
            src_ref=self.out.at[zp],
            dst_ref=self.into.at[source],
            send_sem=self.sent.at[8 + zp],
            recv_sem=self.got.at[8 + source],
            device_id={"head": zp * 4 + self.y * 2 + self.c},
            device_id_type=pl.DeviceIdType.MESH,
        )

    def cross(self, i):
        zp = rem(self.z + turn(i), 8)
        self.side[zp] = encode(self.block(zp, 1 - self.y), self.bound)
        self.pair(zp).start()

    def paired(self, zp):
        total = self.block(zp, self.y)
        self.pair(zp).wait_recv()
        return total + plain(self.other[zp], self.bound)

    def direct(self, i):
        zp = rem(self.z + turn(i), 8)
        self.out[zp] = encode(self.paired(zp), self.bound)
        self.far(zp, self.z).start()

    def finish(self):
        total = self.paired(self.z)
        for j in (1, 7, 2, 6, 3, 5, 4):
            zp = rem(self.z + j, 8)
            self.far(zp, zp).wait_recv()
            total = total + plain(self.into[zp], self.bound)
        return total

    def drain(self):
        @pl.loop(0, 8)
        def _(j):
            self.pair(jnp.int32(j)).wait_send()

        @pl.loop(1, 8)
        def _(j):
            zp = rem(self.z + j, 8)
            self.far(zp, self.z).wait_send()


class Base:
    def __init__(self, place, scratch, fill, before=None):
        self.z, self.y, self.c = place
        self.near, self.far, self.part, self.sent, self.got = scratch
        self.fill, self.before = fill, before
        self.ready = set()

    def core_copy(self, zp):
        return pltpu.make_async_remote_copy(
            src_ref=self.near.at[zp],
            dst_ref=self.far.at[zp],
            send_sem=self.sent.at[zp],
            recv_sem=self.got.at[zp],
            device_id={"head": self.z * 4 + self.y * 2 + 1 - self.c},
            device_id_type=pl.DeviceIdType.MESH,
        )

    def spot(self, i):
        return rem(self.z + turn(i), 8)

    def near_of(self, a, b):
        @pl.loop(a, b)
        def _(i):
            zp = self.spot(i)
            if self.before is not None:
                self.before(zp)
            for yp in range(2):
                self.fill(self.near.at[zp, yp], zp, yp, 1 - self.c)
            self.core_copy(zp).start()

    def own_of(self, a, b):
        @pl.loop(a, b)
        def _(i):
            zp = self.spot(i)
            for yp in range(2):
                self.fill(self.part.at[zp, yp], zp, yp, self.c)

    def need(self, offset):
        zp = rem(self.z + offset, 8)
        if offset not in self.ready:
            self.ready.add(offset)
            self.core_copy(zp).wait_recv()
        return zp

    def drain(self):
        @pl.loop(0, 8)
        def _(i):
            self.core_copy(jnp.int32(i)).wait_send()


class Order:
    def __init__(self, base, lo, hi, bound, scratch):
        self.base, self.lo, self.hi, self.bound = base, lo, hi, bound
        self.z, self.y, self.c = base.z, base.y, base.c
        self.out, self.into, self.side, self.other, self.sent, self.got = scratch
        self.copies = []

    def block(self, zp, yp):
        at = (zp, yp, pl.ds(self.lo, self.hi - self.lo))
        return self.base.part[at] + self.base.far[at]

    def hop(self, at, slot, step):
        return Copies(
            self.out, self.into, at, at, self.sent, self.got, slot, slot,
            {"head": rem(self.z + step, 8) * 4 + self.y * 2 + self.c},
        )

    def pair(self, at, slot):
        return Copies(
            self.side, self.other, at, at, self.sent, self.got, slot, slot,
            {"head": self.z * 4 + (1 - self.y) * 2 + self.c},
        )

    def put(self, ref, at, v):
        ref[at] = encode(v, self.bound)

    def get(self, ref, at):
        return plain(ref[at], self.bound)

    def go(self, copy):
        copy.start()
        self.copies.append(copy)

    def drain(self):
        for copy in self.copies:
            copy.wait_send()


class ZFirst(Order):
    def message(self, side, yp, at):
        return self.hop((side, yp, at), side * 8 + yp * 4 + at, 1 if side else 7)

    def ring(self, t):
        for side in range(2):
            for yp in range(2):
                first = 4 if side == yp else 3
                away = first - t
                if away < 1:
                    continue
                total = self.block(self.base.need((away if side else 8 - away) % 8), yp)
                if away < first:
                    self.message(side, yp, away).wait_recv()
                    total = total + self.get(self.into, (side, yp, away))
                self.put(self.out, (side, yp, away - 1), total)
                self.go(self.message(side, yp, away - 1))

    def gathered(self, yp):
        return self.block(self.z, yp) + self.get(self.into, (0, yp, 0)) + self.get(self.into, (1, yp, 0))

    def across(self):
        self.base.need(0)
        for side in range(2):
            for yp in range(2):
                self.message(side, yp, 0).wait_recv()
        self.put(self.side, 0, self.gathered(1 - self.y))
        self.go(self.pair(0, 16))

    def finish(self):
        total = self.gathered(self.y)
        self.pair(0, 16).wait_recv()
        return total + self.get(self.other, 0)


class YFirst(Order):
    def cross(self, *offsets):
        for offset in offsets:
            zp = self.base.need(offset)
            self.put(self.side, zp, self.block(zp, 1 - self.y))
            self.go(self.pair(zp, 8 + zp))

    def message(self, side, at):
        return self.hop((side, at), side * 4 + at, 1 if side else 7)

    def paired(self, offset):
        zp = rem(self.z + offset, 8)
        total = self.block(zp, self.y)
        self.pair(zp, 8 + zp).wait_recv()
        return total + self.get(self.other, zp)

    def ring(self, t):
        for side in range(2):
            first = 3 if side else 4
            away = first - t
            if away < 1:
                continue
            total = self.paired((away if side else 8 - away) % 8)
            if away < first:
                self.message(side, away).wait_recv()
                total = total + self.get(self.into, (side, away))
            self.put(self.out, (side, away - 1), total)
            self.go(self.message(side, away - 1))

    def finish(self):
        total = self.paired(0)
        for side in range(2):
            self.message(side, 0).wait_recv()
        return total + self.get(self.into, (0, 0)) + self.get(self.into, (1, 0))


def layer(
    pre, dec, w_hbm, lw, swt, up, ow_hbm, start_hbm, gain, rates, biases, skips, at_position, slots, adapter,
    out_pre, out_dec,
    w, ow, start, load, w_sent, w_got, near, far, near_sent, near_got,
    rows, low_part, low_near, low_far, low_sent, low_got,
    owe, owed, owe_sent, owe_got,
    unit, unit_sent, unit_got, pass_sent, pass_got,
    starts, writers, tails, share_sent, share_got,
    begun, weight, norm_pre, norm_dec, base_in, in_pre, in_dec, base_pre, red_pre, base_dec, red_dec,
):
    group, head_at = lax.axis_index("grp"), lax.axis_index("head")
    z, y, c = div(head_at, 4), rem(div(head_at, 2), 2), rem(head_at, 2)
    chip = z * 2 + y
    place = (z, y, c)
    mesh_id = pl.DeviceIdType.MESH

    def columns(block, core):
        return pl.ds(pl.multiple_of((block * 2 + core) * 256, 256), 256)

    def w_own(zp):
        at = pl.ds(pl.multiple_of(zp * 1024, 1024), 1024)
        return pltpu.make_async_copy(w_hbm.at[:, at], w.at[zp], load.at[zp])

    def ow_own(b):
        return pltpu.make_async_copy(ow_hbm.at[:, columns(b, c)], ow.at[b, 0], load.at[16 + b])

    def to_core(source, target, slot):
        return pltpu.make_async_remote_copy(
            src_ref=source,
            dst_ref=target,
            send_sem=w_sent.at[slot],
            recv_sem=w_got.at[slot],
            device_id={"head": chip * 2 + 1 - c},
            device_id_type=mesh_id,
        )

    def ow_other(b):
        return to_core(ow_hbm.at[:, columns(b, 1 - c)], ow.at[b, 1], 16 + b)

    normed_pre_other = to_core(norm_pre.at[0], norm_pre.at[1], 34)
    normed_dec_other = to_core(norm_dec.at[0], norm_dec.at[1], 35)

    @pl.loop(0, 8)
    def _(i):
        w_own(rem(z + turn(i), 8)).start()

    start_copy = pltpu.make_async_copy(start_hbm, start, load.at[32])
    start_copy.start()

    barrier = pltpu.get_barrier_semaphore()

    @pl.loop(1, 16)
    def _(j):
        pl.semaphore_signal(barrier, 1, device_id={"head": rem(chip + j, 16) * 2 + c}, device_id_type=mesh_id)

    @pl.loop(1, 8)
    def _(j):
        pl.semaphore_signal(barrier, 1, device_id={"grp": rem(group + j, 8)}, device_id_type=mesh_id)

    pl.semaphore_signal(barrier, 1, device_id={"head": chip * 2 + 1 - c}, device_id_type=mesh_id)

    @pl.loop(0, 16)
    def _(b):
        ow_own(b).start()

    rows[0:64] = pre[...]
    rows[64:160] = dec[...]
    part = dot(rows[...], lw[...])
    low_part[0] = part[:, 0:256].reshape(10, 16, 256)
    raw = dot(rows[...], swt[...], ((1,), (1,)))
    low_part[1] = jnp.concatenate([part[:, 256:384], raw, jnp.zeros_like(raw)], axis=1).reshape(10, 16, 256)
    low_near[...] = low_part[1 - c]

    spot = iota((64, 128), 0)
    prompt_pre = jnp.where(spot < 32, at_position[2 * group], at_position[2 * group + 1])
    spot = iota((32, 128), 0)
    prompt_dec = jnp.zeros((32, 128), jnp.int32)
    for j in range(32):
        prompt_dec = jnp.where(spot == j, div(slots[j], 16), prompt_dec)
    tenant_pre = jnp.zeros((64, 128), jnp.int32)
    tenant_dec = jnp.zeros((32, 128), jnp.int32)
    where_dec = jnp.full((32, 128), -1, jnp.int32)
    for j in range(16):
        tenant_pre = jnp.where(prompt_pre == j, adapter[j], tenant_pre)
        tenant_dec = jnp.where(prompt_dec == j, adapter[j], tenant_dec)
        where_dec = jnp.where(prompt_dec == at_position[j], j, where_dec)
    tenant_dec = jnp.concatenate([tenant_dec] * 3, axis=0)
    where_dec = jnp.concatenate([where_dec] * 3, axis=0)

    pl.semaphore_wait(barrier, 23)
    low_core = pltpu.make_async_remote_copy(
        src_ref=low_near,
        dst_ref=low_far,
        send_sem=low_sent.at[0],
        recv_sem=low_got.at[0],
        device_id={"head": chip * 2 + 1 - c},
        device_id_type=mesh_id,
    )
    low_core.start()

    def share(ref, kind, source, g):
        return pltpu.make_async_remote_copy(
            src_ref=ref.at[source],
            dst_ref=ref.at[source],
            send_sem=share_sent.at[kind, g],
            recv_sem=share_got.at[kind, source],
            device_id={"grp": g},
            device_id_type=mesh_id,
        )

    def to_groups(ref, kind):
        @pl.loop(1, 8)
        def _(j):
            share(ref, kind, group, rem(group + j, 8)).start()

    def from_groups(ref, kind):
        @pl.loop(1, 8)
        def _(j):
            g = rem(group + j, 8)
            share(ref, kind, g, g).wait_recv()

    def owe_copy(u, source):
        return Copies(
            owe, owed, u, source, owe_sent, owe_got, u, source, {"head": u * 2 + c}
        )

    def unit_copy(k, to):
        return Copies(
            unit, unit, (k, c), (k, c), unit_sent, unit_got, to, k, {"head": to * 2 + c}
        )

    def pass_copy(k, core):
        return Copies(
            unit, unit, (k, core), (k, core), pass_sent, pass_got, k, k,
            {"head": chip * 2 + 1 - c},
        )

    def piece(zp, yp, core):
        at = pl.ds(pl.multiple_of((yp * 2 + core) * 256, 256), 256)
        return dot(rows[...], w[zp, :, at])

    def fill(ref, zp, yp, core):
        ref[...] = piece(zp, yp, core)

    base = Base(place, (near, far, base_in, near_sent, near_got), fill, lambda zp: w_own(zp).wait())
    zs, ys = ZFirst(base, 0, 64, IN_BOUND, in_pre), YFirst(base, 64, 160, IN_BOUND, in_dec)
    base.near_of(0, 3)
    low_core.wait_recv()

    @pl.loop(0, 10)
    def _(u):
        owe[u] = encode(low_part[c, u] + low_far[u], IN_BOUND)

        @pl.when(u != chip)
        def _():
            owe_copy(u, chip).start()

    base.near_of(3, 5)
    base.own_of(0, 3)
    zs.ring(0)
    ys.cross(4, 3)
    base.near_of(5, 8)
    base.own_of(3, 5)
    ys.cross(5, 2)
    ys.ring(0)

    @pl.when(chip < 10)
    def _():
        owed[chip] = owe[chip]
        total = plain(owed[chip], IN_BOUND)
        for j in range(1, 16):
            source = rem(chip + j, 16)
            owe_copy(chip, source).wait_recv()
            total = total + plain(owed[source], IN_BOUND)
        unit[chip, c] = encode(total, IN_BOUND)

        @pl.loop(1, 16)
        def _(j):
            unit_copy(chip, rem(chip + j, 16)).start()

    zs.ring(1)
    base.own_of(5, 8)
    ys.cross(6, 1)
    ys.ring(1)
    ys.cross(7, 0)
    start_copy.wait()
    for i in range(2):
        starts[group, 128 * i : 128 * i + 128] = encode(start[i], START_BOUND)
    to_groups(starts, 0)

    @pl.loop(0, 16)
    def _(b):
        ow_other(b).start()

    zs.ring(2)

    @pl.loop(0, 10)
    def _(k):
        @pl.when(k != chip)
        def _():
            unit_copy(k, chip).wait_recv()

        pass_copy(k, c).start()

    ys.ring(2)
    zs.ring(3)
    ys.ring(3)
    zs.across()

    @pl.loop(0, 10)
    def _(k):
        pass_copy(k, 1 - c).wait_recv()

    lows = jnp.concatenate(
        [plain(unit[:, core], IN_BOUND).reshape(160, 256) for core in range(2)], axis=1
    )
    writers[group] = encode(lows[0:64, 0:128], IN_BOUND)
    to_groups(writers, 1)
    reader_high, reader_rest = split(lows[64:160, 128:256])

    half = iota((1, 128), 1) < 64
    rate = jnp.where(half, rates[0], rates[1])
    bias = jnp.where(half, biases[0], biases[1])
    skip = jnp.where(half, skips[0], skips[1])
    low_pre, low_dec = lows[0:64], lows[64:160]
    values, gate, length, decay = channels(zs.finish(), low_pre, tenant_pre, head_at, up[...], rate, bias)
    running = run(decay)
    carried, last = tail_values(values, length, running)
    tails[group, 0:64] = encode(carried, TAIL_BOUND)
    tails[group, 64:80] = encode(last, 1.0)
    to_groups(tails, 2)
    y_out = prefill(values, length, running, low_pre[:, 0:128], low_pre[:, 128:256], start, skip)
    norm_pre[0] = normalise(y_out, gate, gain[...])
    normed_pre_other.start()

    def spread(reduce, normed):
        both = jnp.concatenate([normed[0], normed[1]], axis=1)

        @pl.loop(0, 8)
        def _(i):
            zp = rem(z + turn(i), 8)
            for yp in range(2):
                reduce.part[zp, yp] = dot(both, ow[zp * 2 + yp].reshape(256, 256))
            reduce.cross(i)

    def forward(reduce):
        @pl.loop(0, 7)
        def _(i):
            reduce.direct(i)

    @pl.loop(0, 16)
    def _(b):
        ow_own(b).wait()
        ow_other(b).wait_recv()

    second = Reduce(place, base_pre, 0, 64, OUT_BOUND, red_pre)
    normed_pre_other.wait_recv()
    spread(second, norm_pre)
    values, gate, length, decay = channels(ys.finish(), low_dec, tenant_dec, head_at, up[...], rate, bias)
    from_groups(starts, 0)
    pick = jnp.zeros((96, 128), F32)
    for g in range(8):
        both = dot3((reader_high, reader_rest), split(plain(starts[g], START_BOUND)), ((1,), (1,)))
        pick = jnp.where(where_dec == 2 * g, both[:, 0:128], pick)
        pick = jnp.where(where_dec == 2 * g + 1, both[:, 128:256], pick)
    begun[...] = pick
    from_groups(writers, 1)
    scores = dot3(
        (reader_high, reader_rest), split(plain(writers[...], IN_BOUND).reshape(512, 128)), ((1,), (1,))
    )
    spot = jnp.concatenate([where_dec] * 4, axis=1)
    weight[...] = jnp.where(spot == iota((96, 512), 1) // 32, scores, 0.0)
    y_own, grown = decode(values, length, decay, low_dec[:, 0:128], low_dec[:, 128:256], skip)

    forward(second)
    from_groups(tails, 2)
    scaled = jnp.zeros((96, 128), F32)
    for i in range(16):
        grown_i = plain(tails[i // 2, 64:80], 1.0)[8 * (i % 2) : 8 * (i % 2) + 1]
        scaled = jnp.where(where_dec == i, grown_i, scaled)
    carried = plain(tails[:, 0:64], TAIL_BOUND).reshape(512, 128)
    seen = scaled * begun[...] + dot3(split(weight[...]), split(carried))
    norm_dec[0] = normalise(y_own + grown * seen, gate, gain[...])
    normed_dec_other.start()
    third = Reduce(place, base_dec, 0, 96, OUT_BOUND, red_dec)
    normed_dec_other.wait_recv()
    spread(third, norm_dec)
    forward(third)
    out_pre[...] = second.finish()
    out_dec[...] = third.finish()

    for reduce in (base, zs, ys, second, third):
        reduce.drain()
    for copy in (normed_pre_other, normed_dec_other):
        copy.wait_send()

    @pl.loop(0, 16)
    def _(b):
        ow_other(b).wait_send()

    low_core.wait_send()

    @pl.loop(0, 10)
    def _(k):
        @pl.when(k != chip)
        def _():
            owe_copy(k, chip).wait_send()

        pass_copy(k, c).wait_send()

    @pl.when(chip < 10)
    def _():
        @pl.loop(1, 16)
        def _(j):
            unit_copy(chip, rem(chip + j, 16)).wait_send()

    @pl.loop(1, 8)
    def _(j):
        g = rem(group + j, 8)
        share(starts, 0, group, g).wait_send()
        share(writers, 1, group, g).wait_send()
        share(tails, 2, group, g).wait_send()


def add_rows(pre, dec, sum_pre, sum_dec, out_pre, out_dec):
    out_pre[...] = pre[...].astype(F32) + sum_pre[...]
    out_dec[...] = dec[...].astype(F32) + sum_dec[...]


def coded(*lead, rows):
    return [pltpu.VMEM((*lead, rows, 256), jnp.int16)]


def base_scratch(rows):
    return pltpu.VMEM((8, 2, rows, 256), F32)


def z_scratch(rows):
    return coded(2, 2, 4, rows=rows) * 2 + coded(1, rows=rows) * 2 + [pltpu.SemaphoreType.DMA((17,))] * 2


def y_scratch(rows):
    return coded(2, 4, rows=rows) * 2 + coded(8, rows=rows) * 2 + [pltpu.SemaphoreType.DMA((16,))] * 2


def reduce_scratch(rows):
    return coded(8, rows=rows) * 4 + [pltpu.SemaphoreType.DMA((16,))] * 2


def on_device(pre, dec, w, lw, sw, up, ow, rate, bias, skip, gain, start, at_position, slots, adapter):
    vmem = pl.BlockSpec(memory_space=pltpu.VMEM)
    smem = pl.BlockSpec(memory_space=pltpu.SMEM)
    any_ = pl.BlockSpec(memory_space=pltpu.HBM)
    dma = pltpu.SemaphoreType.DMA
    dec = dec.reshape(96, 256)
    sum_pre, sum_dec = pl.pallas_call(
        layer,
        out_shape=(jax.ShapeDtypeStruct((64, 256), F32), jax.ShapeDtypeStruct((96, 256), F32)),
        in_specs=[vmem, vmem, any_, vmem, vmem, vmem, any_, any_, vmem] + [smem] * 6,
        out_specs=(vmem, vmem),
        scratch_shapes=[
            pltpu.VMEM((8, 256, 1024), jnp.bfloat16),
            pltpu.VMEM((16, 2, 128, 256), jnp.bfloat16),
            pltpu.VMEM((2, 128, 128), F32),
            dma((33,)),
            dma((36,)),
            dma((36,)),
            pltpu.VMEM((8, 2, 160, 256), F32),
            pltpu.VMEM((8, 2, 160, 256), F32),
            dma((8,)),
            dma((8,)),
            pltpu.VMEM((160, 256), jnp.bfloat16),
            pltpu.VMEM((2, 10, 16, 256), F32),
            pltpu.VMEM((10, 16, 256), F32),
            pltpu.VMEM((10, 16, 256), F32),
            dma((1,)),
            dma((1,)),
            *coded(10, rows=16),
            *coded(16, rows=16),
            dma((10,)),
            dma((16,)),
            *coded(10, 2, rows=16),
            dma((16,)),
            dma((10,)),
            dma((10,)),
            dma((10,)),
            pltpu.VMEM((8, 256, 128), jnp.int16),
            pltpu.VMEM((8, 64, 128), jnp.int16),
            pltpu.VMEM((8, 80, 128), jnp.int16),
            dma((3, 8)),
            dma((3, 8)),
            pltpu.VMEM((96, 128), F32),
            pltpu.VMEM((96, 512), F32),
            pltpu.VMEM((2, 64, 128), jnp.bfloat16),
            pltpu.VMEM((2, 96, 128), jnp.bfloat16),
            base_scratch(160),
            z_scratch(64),
            y_scratch(96),
            base_scratch(64),
            reduce_scratch(64),
            base_scratch(96),
            reduce_scratch(96),
        ],
        compiler_params=pltpu.CompilerParams(
            collective_id=0, has_side_effects=True, vmem_limit_bytes=60 * 1024 * 1024
        ),
        name="layer",
    )(
        pre, dec, w, lw, sw.T, up, ow, start.reshape(2, 128, 128), gain[None], rate, bias, skip,
        at_position, slots, adapter,
    )
    out_pre, out_dec = pl.pallas_call(
        add_rows,
        out_shape=(jax.ShapeDtypeStruct((64, 256), F32), jax.ShapeDtypeStruct((96, 256), F32)),
        name="add_rows",
    )(pre, dec, sum_pre, sum_dec)
    return out_pre, out_dec.reshape(3, 32, 256)


def solution(mesh):
    placed = (
        P("grp", "head"),
        P(None, "grp", "head"),
        P("head", None),
        P("head", None),
        P("head", None),
        P(None, "head"),
        P("head", None),
        P("head"),
        P("head"),
        P("head"),
        P("head"),
        P("grp", "head", None, None),
        P(),
        P("grp"),
        P(),
    )
    return jax.shard_map(
        on_device,
        mesh=mesh,
        in_specs=placed,
        out_specs=(P("grp", "head"), P(None, "grp", "head")),
        check_vma=False,
    )
```
